128 devices in a mesh: ctx: 32 (over y, z, core), head: 4 (over x).
Axes of the slice: x: 4, y: 4, z: 4, core: 2. Of those that a mesh axis runs over, the one named last changes fastest.
Arguments:
- stream: bfloat16 [16384, 2048], P(('ctx', 'head')), may hold values from -6 to 6
- moe_gain: float32 [2048], replicated, may hold values from 0.5 to 1.5
- router: bfloat16 [2048, 256], replicated, may hold values from -0.125 to 0.125
- expert_ids: int32 [16384, 10], P(('ctx', 'head')), may hold values from 0 to 255, all different within a row; in each aligned block of 128 rows (0 to 127, 128 to 255, ...) at most 6 rows name the same one
- expert_gate: bfloat16 [256, 2048, 512], P(('ctx', 'head')), may hold values from -0.125 to 0.125
- expert_up: bfloat16 [256, 2048, 512], P(('ctx', 'head')), may hold values from -0.125 to 0.125
- expert_down: bfloat16 [256, 512, 2048], P(('ctx', 'head')), may hold values from -1 to 1
- mixer_gain: float32 [2048], replicated, may hold values from 0.5 to 1.5
- query_weight: bfloat16 [2048, 1024], P(None, 'head'), may hold values from -0.125 to 0.125
- key_weight: bfloat16 [2048, 1024], P(None, 'head'), may hold values from -0.125 to 0.125
- value_weight: bfloat16 [2048, 2048], P(None, 'head'), may hold values from -0.125 to 0.125
- output_gate: bfloat16 [2048, 2048], P(None, 'head'), may hold values from -0.125 to 0.125
- beta_weight: bfloat16 [2048, 16], P(None, 'head'), may hold values from -0.125 to 0.125
- decay_weight: bfloat16 [2048, 16], P(None, 'head'), may hold values from -0.5 to 0.5
- query_conv: float32 [4, 1024], P(None, 'head'), may hold values from -3 to 3
- key_conv: float32 [4, 1024], P(None, 'head'), may hold values from -3 to 3
- value_conv: float32 [4, 2048], P(None, 'head'), may hold values from -3 to 3
- decay_log: float32 [16], P('head'), may hold values from -12 to -2.5
- decay_bias: float32 [16], P('head'), may hold values from -2 to 1
- head_gain: float32 [128], replicated, may hold values from 0.5 to 1.5
- out_weight: bfloat16 [2048, 2048], P('head'), may hold values from -0.125 to 0.125
Outputs:
- moe_out: bfloat16 [16384, 2048], P(('ctx', 'head'))
- mixer_out: bfloat16 [16384, 2048], P(('ctx', 'head'))
The draws below stay inside these ranges and needn't reach their ends.
Inputs may be any that keep to these rules, and one draw needn't show every extreme that they name: `expert_ids`: each row names 10 different experts; in each aligned block of 128 rows (the rows of one device) no expert is named by more than 6 rows, a bound that some block reaches.
All inputs are finite; a program needn't handle non-finite values.
Results may differ from the reference program's by a relative error of at most 0.017.
Values may be sent and summed in bfloat16 or wider, within the bound.
A program may use at most 128 MiB of HBM per device.

```python
import math
import jax
import jax.numpy as jnp
import numpy as np
from jax import lax

D = 2048
EH = 512
VH = 16
KH = 8
DK = 128
DV = 128
TOPK = 10
KCONV = 4
TOK_DEV = 128
EXPERTS = 256
CAP = 6
TOKENS = 16384
N_CTX = 32
N_HEAD = 4


def draw_decay_log(key, part):
    drawn = jax.random.uniform(key, (VH,), jnp.float32, -11.0, -2.5)
    return drawn


def steps_of(key, extent, pieces, smallest, largest):
    level = 1.0
    for position, blocks in pieces:
        steps = jax.random.uniform(jax.random.fold_in(jax.random.fold_in(key, 6), position), (blocks,), jnp.float32, smallest / len(pieces), largest / len(pieces))
        level = level * jnp.repeat(jnp.exp(steps), extent[position] // blocks).reshape((-1,) + (1,) * (len(extent) - 1 - position))
    return level


def routed_block(rng, own, number, rows, count, top, most, skew):
    sequence = jax.random.permutation(rng, count)
    heavy_load, ordinary = shares(count, rows * top, most, skew, True), shares(count, rows * top, most, skew, False)
    places = jnp.arange(count)

    def named(tallies, offset_by):
        used = int((tallies > 0).sum())
        fixed = max(1, used // 4)
        moved = fixed + (places - fixed + offset_by * (used - fixed)) % max(1, count - fixed)
        return jnp.zeros((count,), jnp.int32).at[sequence[jnp.where(places < fixed, places, moved)]].set(jnp.asarray(tallies, jnp.int32))

    tallies = jnp.where(number % 4 == 0, named(heavy_load, number // 4), named(ordinary, number - number // 4 - 1))
    mixed = jax.random.permutation(jax.random.fold_in(own, 3), count)
    source_of, sink = mixed[0:count // 2 * 2:2], mixed[1:count // 2 * 2:2]
    slack = jnp.minimum(tallies[source_of] - 1, most - tallies[sink]) // 2
    slack = jnp.where((source_of == sequence[0]) | (sink == sequence[0]) | (tallies[sink] == 0), 0, jnp.maximum(slack, 0))
    moved = jax.random.randint(jax.random.fold_in(own, 4), (count // 2,), 0, 1 << 20) % (slack + 1)
    tallies = tallies.at[source_of].add(-moved).at[sink].add(moved)
    members = jnp.searchsorted(jnp.cumsum(tallies), jnp.arange(rows * top), side="right").astype(jnp.int32)
    table = members.reshape(top, rows).T
    table = table[jax.random.permutation(jax.random.fold_in(own, 1), rows)]
    offset_by = jax.random.randint(jax.random.fold_in(own, 2), (rows, 1), 0, top)
    return jnp.take_along_axis(table, (jnp.arange(top)[None, :] + offset_by) % top, axis=1)


def shares(number_of, total, reach, skew, full):
    loads = [(1 << 20) // math.isqrt(standing ** skew) + 1 for standing in range(1, number_of + 1)]
    largest = reach if full else min(reach, max(-(-total // number_of), total * loads[0] // sum(loads)))
    least = 1 if total - largest >= number_of - 1 else 0
    given, surplus = [largest] + [least] * (number_of - 1), total - largest - least * (number_of - 1)
    while surplus > 0:
        movable = [i for i in range(1, number_of) if given[i] < largest] or [i for i in range(1, number_of) if given[i] < reach]
        whole, left = sum([loads[i] for i in movable]), surplus
        for i in movable:
            addition = min(reach - given[i], max(1, left * loads[i] // whole), surplus)
            given[i] = given[i] + addition
            surplus = surplus - addition
    return np.array(given)


def bell_draw(stream_key, shape, deviation, reach, cuts=(), kind=jnp.bfloat16):
    level = steps_of(stream_key, shape, cuts, -0.22, 0.18) if cuts else 1.0
    entries = jax.random.normal(stream_key, shape, jnp.float32) * deviation * level
    return jnp.minimum(jnp.maximum(entries, -reach), reach).astype(kind)


def setup_inputs(seed: int = 0) -> dict:
    streams_of = jax.random.split(jax.random.key(seed), 22)
    stream = bell_draw(streams_of[0], (TOKENS, D), 1.0, 6.0, ((0, 128),))
    moe_gain = jnp.clip(1.0 + 0.1 * jax.random.normal(streams_of[1], (D,), jnp.float32), 0.5, 1.5)
    router = bell_draw(streams_of[2], (D, EXPERTS), D ** -0.5, 0.125)
    expert_ids_keys = jax.random.split(jax.random.fold_in(streams_of[3], 1), TOKENS // TOK_DEV)
    expert_ids_turns = jax.random.permutation(jax.random.fold_in(streams_of[3], 3), TOKENS // TOK_DEV)
    expert_ids = jax.vmap(lambda own, number: routed_block(jax.random.fold_in(streams_of[3], 2), own, number, TOK_DEV, EXPERTS, TOPK, CAP, 1))(expert_ids_keys, expert_ids_turns).reshape((TOKENS, TOPK))
    expert_gate = bell_draw(streams_of[4], (EXPERTS, D, EH), D ** -0.5, 0.125, ((0, 128),))
    expert_up = bell_draw(streams_of[5], (EXPERTS, D, EH), D ** -0.5, 0.125, ((0, 128),))
    expert_down = bell_draw(streams_of[6], (EXPERTS, EH, D), (EH // 16) ** -0.5, 1.0, ((0, 128),))
    mixer_gain = jnp.clip(1.0 + 0.1 * jax.random.normal(streams_of[7], (D,), jnp.float32), 0.5, 1.5)
    query_weight = bell_draw(streams_of[8], (D, KH * DK), D ** -0.5, 0.125, ((1, 4),))
    key_weight = bell_draw(streams_of[9], (D, KH * DK), D ** -0.5, 0.125, ((1, 4),))
    value_weight = bell_draw(streams_of[10], (D, VH * DV), D ** -0.5, 0.125, ((1, 4),))
    output_gate = bell_draw(streams_of[11], (D, VH * DV), D ** -0.5, 0.125, ((1, 4),))
    beta_weight = bell_draw(streams_of[12], (D, VH), D ** -0.5, 0.125, ((1, 4),))
    decay_weight = bell_draw(streams_of[13], (D, VH), (D // 16) ** -0.5, 0.5, ((1, 4),))
    query_conv = bell_draw(streams_of[14], (KCONV, KH * DK), 0.5, 3.0, ((1, 4),), jnp.float32)
    key_conv = bell_draw(streams_of[15], (KCONV, KH * DK), 0.5, 3.0, ((1, 4),), jnp.float32)
    value_conv = bell_draw(streams_of[16], (KCONV, VH * DV), 0.5, 3.0, ((1, 4),), jnp.float32)
    decay_log = draw_decay_log(jax.random.fold_in(streams_of[21], 71), 0)
    decay_bias = jnp.clip(-2.0 + 3.0 * jax.random.uniform(streams_of[18], (VH,), jnp.float32) ** steps_of(streams_of[18], (VH,), ((0, 4),), -0.2, 0.2), -2.0, 1.0)
    head_gain = jnp.clip(1.0 + 0.1 * jax.random.normal(streams_of[19], (DV,), jnp.float32), 0.5, 1.5)
    out_weight = bell_draw(streams_of[20], (VH * DV, D), (VH * DV) ** -0.5, 0.125, ((0, 4),))
    return dict(stream=stream, moe_gain=moe_gain, router=router, expert_ids=expert_ids, expert_gate=expert_gate, expert_up=expert_up, expert_down=expert_down, mixer_gain=mixer_gain, query_weight=query_weight, key_weight=key_weight, value_weight=value_weight, output_gate=output_gate, beta_weight=beta_weight, decay_weight=decay_weight, query_conv=query_conv, key_conv=key_conv, value_conv=value_conv, decay_log=decay_log, decay_bias=decay_bias, head_gain=head_gain, out_weight=out_weight)


epsilon = 1e-06
exact_precision = lax.Precision.HIGHEST

def rms_rows(values, gain):
    values = values.astype(jnp.float32)
    scale = lax.rsqrt(lax.optimization_barrier(jnp.mean(values * values, axis=-1, keepdims=True)) + epsilon)
    return values * scale * gain.astype(jnp.float32)

def block_terms(queries, key_rows, values, strength, decays):
    length = queries.shape[0]
    cumulative = jnp.cumsum(decays)
    spread = cumulative[:, None] - cumulative[None, :]
    positions = jnp.arange(length, dtype=jnp.int32)
    strict = positions[:, None] > positions[None, :]
    inclusive = positions[:, None] >= positions[None, :]
    fall_strict = jnp.where(strict, jnp.exp(jnp.where(strict, spread, 0.0)), 0.0)
    fall_inclusive = jnp.where(inclusive, jnp.exp(jnp.where(inclusive, spread, 0.0)), 0.0)
    key_dots = jnp.dot(key_rows, key_rows.T, precision=exact_precision)
    strict_part = strength[:, None] * fall_strict * key_dots
    system = jnp.eye(length, dtype=jnp.float32) + strict_part
    targets = strength[:, None] * jnp.concatenate([values, jnp.exp(cumulative)[:, None] * key_rows], axis=1)
    solved = jax.scipy.linalg.solve_triangular(system, targets, lower=True, unit_diagonal=True)
    value_width = values.shape[1]
    w_values = solved[:, :value_width]
    w_keys = solved[:, value_width:]
    mixing = fall_inclusive * jnp.dot(queries, key_rows.T, precision=exact_precision)
    q_decayed = jnp.exp(cumulative)[:, None] * queries
    k_decayed = jnp.exp(cumulative[-1] - cumulative)[:, None] * key_rows
    closing = jnp.exp(cumulative[-1])
    return (w_values, w_keys, mixing, q_decayed, k_decayed, closing)

def delta_head(queries, key_rows, values, strength, decays):
    length = queries.shape[0]
    block_len = math.gcd(length, 64)
    block_count = length // block_len

    def split_blocks(array):
        return array.reshape((block_count, block_len) + array.shape[1:])
    terms = jax.vmap(block_terms)(split_blocks(queries), split_blocks(key_rows), split_blocks(values), split_blocks(strength), split_blocks(decays))

    def advance(state_now, block_term):
        w_values, w_keys, mixing, q_decayed, k_decayed, closing = block_term
        update = w_values - jnp.dot(w_keys, state_now, precision=exact_precision)
        result = jnp.dot(q_decayed, state_now, precision=exact_precision) + jnp.dot(mixing, update, precision=exact_precision)
        state_now = closing * state_now + jnp.dot(k_decayed.T, update, precision=exact_precision)
        return (state_now, result)
    initial = jnp.zeros((key_rows.shape[1], values.shape[1]), jnp.float32)
    final_state, results = lax.scan(advance, initial, terms)
    return results.reshape(length, values.shape[1])

def unit_heads(array, heads):
    reshaped_rows = array.reshape(array.shape[0], heads, -1)
    return reshaped_rows * lax.rsqrt(lax.optimization_barrier(jnp.sum(reshaped_rows * reshaped_rows, axis=-1, keepdims=True)) + epsilon)

def causal_conv(raw_rows, taps):
    row_count = raw_rows.shape[0]
    extended = jnp.concatenate([jnp.zeros((KCONV - 1, raw_rows.shape[1]), jnp.float32), raw_rows.astype(jnp.float32)], axis=0)
    summed = jnp.zeros((row_count, raw_rows.shape[1]), jnp.float32)
    for shift_index in range(KCONV):
        summed = summed + taps[shift_index][None, :] * extended[shift_index:shift_index + row_count]
    return jax.nn.silu(summed)

def reference(stream, moe_gain, router, expert_ids, expert_gate, expert_up, expert_down, mixer_gain, query_weight, key_weight, value_weight, output_gate, beta_weight, decay_weight, query_conv, key_conv, value_conv, decay_log, decay_bias, head_gain, out_weight):
    sources = N_CTX * N_HEAD
    normed = rms_rows(stream, moe_gain).astype(jnp.bfloat16)
    logits = jnp.dot(normed.astype(jnp.float32), router.astype(jnp.float32), preferred_element_type=jnp.float32)
    chosen = jnp.take_along_axis(logits, expert_ids, axis=1)
    raised = jnp.exp(chosen)
    weights = raised / lax.optimization_barrier(jnp.sum(raised, axis=1, keepdims=True))
    block_ids = expert_ids.reshape(sources, TOK_DEV * TOPK)

    def rank_block(ids_row):
        matches = (ids_row[:, None] == jnp.arange(EXPERTS, dtype=jnp.int32)[None, :]).astype(jnp.int32)
        ranks = jnp.cumsum(matches, axis=0) - 1
        return lax.optimization_barrier(jnp.sum(ranks * matches, axis=1)).astype(jnp.int32)
    slot_index = lax.map(rank_block, block_ids)
    source_index = jnp.arange(sources, dtype=jnp.int32)[:, None]
    places = (block_ids * (sources * CAP) + source_index * CAP + slot_index).reshape(-1).astype(jnp.int32)
    token_index = (jnp.arange(TOKENS * TOPK, dtype=jnp.int32) // TOPK).astype(jnp.int32)
    slot_table = jnp.full((EXPERTS * sources * CAP,), TOKENS, jnp.int32).at[places].set(token_index)
    slot_weights = jnp.zeros((EXPERTS * sources * CAP,), jnp.float32).at[places].set(weights.reshape(-1))
    padded = jnp.concatenate([normed, jnp.zeros((1, D), jnp.bfloat16)], axis=0)

    def one_expert(summed, packed):
        row_index, row_weights, gate_matrix, up_matrix, down_matrix = packed
        inputs = padded[row_index]
        gate_part = jnp.dot(inputs.astype(jnp.float32), gate_matrix.astype(jnp.float32), preferred_element_type=jnp.float32)
        up_part = jnp.dot(inputs.astype(jnp.float32), up_matrix.astype(jnp.float32), preferred_element_type=jnp.float32)
        hidden = (jax.nn.silu(gate_part) * up_part).astype(jnp.bfloat16)
        output_list = jnp.dot(hidden.astype(jnp.float32), down_matrix.astype(jnp.float32), preferred_element_type=jnp.float32).astype(jnp.bfloat16)
        summed = summed.at[row_index].add(row_weights[:, None] * output_list.astype(jnp.float32))
        return (summed, None)
    start_sum = jnp.zeros((TOKENS + 1, D), jnp.float32)
    summed, unused = lax.scan(one_expert, start_sum, (slot_table.reshape(EXPERTS, sources * CAP), slot_weights.reshape(EXPERTS, sources * CAP), expert_gate, expert_up, expert_down))
    moe_out = summed[:TOKENS].astype(jnp.bfloat16)
    mixer_in = rms_rows(stream.astype(jnp.float32) + moe_out.astype(jnp.float32), mixer_gain).astype(jnp.bfloat16)
    query_raw = jnp.dot(mixer_in.astype(jnp.float32), query_weight.astype(jnp.float32), preferred_element_type=jnp.float32).astype(jnp.bfloat16)
    key_raw = jnp.dot(mixer_in.astype(jnp.float32), key_weight.astype(jnp.float32), preferred_element_type=jnp.float32).astype(jnp.bfloat16)
    value_raw = jnp.dot(mixer_in.astype(jnp.float32), value_weight.astype(jnp.float32), preferred_element_type=jnp.float32).astype(jnp.bfloat16)
    gate_raw = jnp.dot(mixer_in.astype(jnp.float32), output_gate.astype(jnp.float32), preferred_element_type=jnp.float32).astype(jnp.bfloat16)
    beta_raw = jnp.dot(mixer_in.astype(jnp.float32), beta_weight.astype(jnp.float32), preferred_element_type=jnp.float32)
    decay_raw = jnp.dot(mixer_in.astype(jnp.float32), decay_weight.astype(jnp.float32), preferred_element_type=jnp.float32)
    queries = unit_heads(causal_conv(query_raw, query_conv), KH) * DK ** (-0.5)
    key_rows = unit_heads(causal_conv(key_raw, key_conv), KH)
    values = causal_conv(value_raw, value_conv).reshape(TOKENS, VH, DV)
    strength = jax.nn.sigmoid(beta_raw)
    decays = -jnp.exp(decay_log)[None, :] * jax.nn.softplus(decay_raw + decay_bias[None, :])
    group_size = VH // KH
    query_heads = jnp.repeat(queries, group_size, axis=1).transpose(1, 0, 2)
    key_heads = jnp.repeat(key_rows, group_size, axis=1).transpose(1, 0, 2)

    def run_head(packed):
        return delta_head(packed[0], packed[1], packed[2], packed[3], packed[4])
    delta_core_output = lax.map(run_head, (query_heads, key_heads, values.transpose(1, 0, 2), strength.T, decays.T))
    delta_core_output = delta_core_output.transpose(1, 0, 2)
    normal = delta_core_output * lax.rsqrt(lax.optimization_barrier(jnp.mean(delta_core_output * delta_core_output, axis=-1, keepdims=True)) + epsilon) * head_gain
    gate_values = gate_raw.astype(jnp.float32).reshape(TOKENS, VH, DV)
    gated_out = (normal * jax.nn.silu(gate_values)).astype(jnp.bfloat16).reshape(TOKENS, VH * DV)
    mixer_out = jnp.dot(gated_out.astype(jnp.float32), out_weight.astype(jnp.float32), preferred_element_type=jnp.float32).astype(jnp.bfloat16)
    return (moe_out, mixer_out)
```

```python
import math

import jax
import jax.numpy as jnp
from jax import lax
from jax.experimental import pallas as pl
from jax.experimental.pallas import tpu as pltpu
from jax.sharding import PartitionSpec as P

DK = 128
HI = lax.Precision.HIGHEST
CHUNK = 64


def _mm(a, b):
    return jnp.dot(a, b, precision=HI, preferred_element_type=jnp.float32)


def _mm_nt(a, b):
    return lax.dot_general(a, b, (((1,), (1,)), ((), ())), precision=HI,
                           preferred_element_type=jnp.float32)


def _mm_tn(a, b):
    return lax.dot_general(a, b, (((0,), (0,)), ((), ())), precision=HI,
                           preferred_element_type=jnp.float32)


def delta_kernel(q_ref, k_ref, v_ref, b_ref, cc_ref, cr_ref, res_ref, read_ref, t_ref, o_ref):
    length, kw = q_ref.shape[1], q_ref.shape[2]
    vw = v_ref.shape[2]
    n_chunks = length // CHUNK
    row = lax.broadcasted_iota(jnp.int32, (CHUNK, CHUNK), 0)
    col = lax.broadcasted_iota(jnp.int32, (CHUNK, CHUNK), 1)
    strict = row > col
    inclusive = row >= col
    eye_c = jnp.where(row == col, 1.0, 0.0).astype(jnp.float32)
    krow = lax.broadcasted_iota(jnp.int32, (kw, kw), 0)
    kcol = lax.broadcasted_iota(jnp.int32, (kw, kw), 1)
    eye_k = jnp.where(krow == kcol, 1.0, 0.0).astype(jnp.float32)

    def body(c, carry):
        state, transfer = carry
        rows = pl.ds(pl.multiple_of(c * CHUNK, CHUNK), CHUNK)
        q = q_ref[0, rows, :]
        k = k_ref[0, rows, :]
        v = v_ref[0, rows, :]
        beta = b_ref[0, rows, :]
        cum_c = cc_ref[0, rows, :]
        cum_r = cr_ref[0, pl.ds(c, 1), :]
        spread = cum_c - cum_r
        fall_s = jnp.where(strict, jnp.exp(jnp.where(strict, spread, 0.0)), 0.0)
        fall_i = jnp.where(inclusive, jnp.exp(jnp.where(inclusive, spread, 0.0)), 0.0)
        a = beta * fall_s * _mm_nt(k, k)
        inv = eye_c
        size = 1
        while size < CHUNK:
            band = ((row // (2 * size)) == (col // (2 * size))) & ((row // size) != (col // size))
            e = jnp.where(band, a, 0.0)
            inv = inv - _mm(_mm(inv, e), inv)
            size *= 2
        ec = jnp.exp(cum_c)
        w_values = _mm(inv, beta * v)
        w_keys = _mm(inv, (beta * ec) * k)
        mixing = fall_i * _mm_nt(q, k)
        q_dec = ec * q
        last = cum_r[:, CHUNK - 1:CHUNK]
        k_dec = jnp.exp(last - cum_c) * k
        closing = jnp.exp(last)
        update = w_values - _mm(w_keys, state)
        res_ref[0, rows, :] = _mm(q_dec, state) + _mm(mixing, update)
        moved = _mm(w_keys, transfer)
        read_ref[0, rows, :] = _mm(q_dec, transfer) - _mm(mixing, moved)
        state = closing * state + _mm_tn(k_dec, update)
        transfer = closing * transfer - _mm_tn(k_dec, moved)
        return state, transfer

    state0 = jnp.zeros((kw, vw), jnp.float32)
    state, transfer = lax.fori_loop(0, n_chunks, body, (state0, eye_k))
    t_ref[0] = transfer
    o_ref[0] = state


def local_delta(queries, key_rows, values, strength, decays):
    heads, length, kw = queries.shape
    vw = values.shape[2]
    n_chunks = length // CHUNK
    cum = jnp.cumsum(decays.reshape(heads, n_chunks, CHUNK), axis=-1)
    cum_col = cum.reshape(heads, length, 1)
    beta_col = strength.reshape(heads, length, 1)
    seq = lambda w: pl.BlockSpec((1, length, w), lambda h: (h, 0, 0))
    mat = pl.BlockSpec((1, kw, vw), lambda h: (h, 0, 0))
    return pl.pallas_call(
        delta_kernel,
        grid=(heads,),
        in_specs=[seq(kw), seq(kw), seq(vw), seq(1), seq(1),
                  pl.BlockSpec((1, n_chunks, CHUNK), lambda h: (h, 0, 0))],
        out_specs=[seq(vw), seq(vw), mat, mat],
        out_shape=[jax.ShapeDtypeStruct((heads, length, vw), jnp.float32),
                   jax.ShapeDtypeStruct((heads, length, vw), jnp.float32),
                   jax.ShapeDtypeStruct((heads, kw, vw), jnp.float32),
                   jax.ShapeDtypeStruct((heads, kw, vw), jnp.float32)],
        name="delta_chunks",
    )(queries, key_rows, values, beta_col, cum_col, cum)


epsilon = 1e-06
exact_precision = lax.Precision.HIGHEST


def passed_along(value, axis, steps):
    count = lax.axis_size(axis)
    first, last = (max(0, -steps), min(count, count - steps))
    return lax.ppermute(value, axis, [(source, source + steps) for source in range(first, last)])


def shifted(value, axis, steps):
    count = lax.axis_size(axis)
    return lax.ppermute(value, axis, [(source, source + steps) for source in range(count - steps)])


def batched_mm(a, b):
    return jnp.einsum("hij,hjk->hik", a, b, precision=HI)


def incoming_state(transfer, offset, axis):
    count, place = lax.axis_size(axis), lax.axis_index(axis)
    steps = 1
    while steps < count:
        far_offset = shifted(offset, axis, steps)
        reached = place >= steps
        if 2 * steps < count:
            far_transfer = shifted(transfer, axis, steps)
            offset = jnp.where(reached, offset + batched_mm(transfer, far_offset), offset)
            transfer = jnp.where(reached, batched_mm(transfer, far_transfer), transfer)
        else:
            offset = jnp.where(reached, offset + batched_mm(transfer, far_offset), offset)
        steps *= 2
    return shifted(offset, axis, 1)


def rms_rows(values, gain):
    values = values.astype(jnp.float32)
    scale = lax.rsqrt(jnp.mean(values * values, axis=-1, keepdims=True) + epsilon)
    return values * scale * gain


def unit_heads(array, heads):
    reshaped_rows = array.reshape(array.shape[0], heads, -1)
    return reshaped_rows * lax.rsqrt(
        jnp.sum(reshaped_rows * reshaped_rows, axis=-1, keepdims=True) + epsilon
    )


def on_device(
    stream,
    moe_gain,
    router,
    expert_ids,
    expert_gate,
    expert_up,
    expert_down,
    mixer_gain,
    query_weight,
    key_weight,
    value_weight,
    output_gate,
    beta_weight,
    decay_weight,
    query_conv,
    key_conv,
    value_conv,
    decay_log,
    decay_bias,
    head_gain,
    out_weight,
):
    ctx_count = lax.axis_size("ctx")
    head_count = lax.axis_size("head")
    sources = ctx_count * head_count
    tok_rows, model_width = stream.shape
    top_count = expert_ids.shape[1]
    local_experts = expert_gate.shape[0]
    experts_all = local_experts * sources
    capacity = (11 * tok_rows * top_count + 10 * experts_all - 1) // (10 * experts_all)
    normed = rms_rows(stream, moe_gain).astype(jnp.bfloat16)
    logits = jnp.dot(normed, router, preferred_element_type=jnp.float32)
    chosen = jnp.take_along_axis(logits, expert_ids, axis=1)
    raised = jnp.exp(chosen)
    weights = raised / jnp.sum(raised, axis=1, keepdims=True)
    flat_ids = expert_ids.reshape(-1)
    matches = (flat_ids[:, None] == jnp.arange(experts_all, dtype=jnp.int32)[None, :]).astype(
        jnp.int32
    )
    slot_index = jnp.sum((jnp.cumsum(matches, axis=0) - 1) * matches, axis=1)
    places = flat_ids * capacity + slot_index
    token_rows = jnp.arange(tok_rows * top_count, dtype=jnp.int32) // top_count
    outgoing = (
        jnp.zeros((experts_all * capacity, model_width), jnp.bfloat16)
        .at[places]
        .set(normed[token_rows])
    )
    outgoing = outgoing.reshape(sources, local_experts, capacity, model_width)
    received = lax.all_to_all(outgoing, ("ctx", "head"), split_axis=0, concat_axis=0, tiled=True)
    gate_part = jnp.einsum(
        "nesd,edh->nesh", received, expert_gate, preferred_element_type=jnp.float32
    )
    up_part = jnp.einsum("nesd,edh->nesh", received, expert_up, preferred_element_type=jnp.float32)
    hidden = (jax.nn.silu(gate_part) * up_part).astype(jnp.bfloat16)
    returned = lax.all_to_all(
        jnp.einsum(
            "nesh,ehd->nesd", hidden, expert_down, preferred_element_type=jnp.float32
        ).astype(jnp.bfloat16),
        ("ctx", "head"),
        split_axis=0,
        concat_axis=0,
        tiled=True,
    )
    gathered_rows = returned.reshape(experts_all * capacity, model_width)[places].reshape(
        tok_rows, top_count, model_width
    )
    moe_out = jnp.sum(weights[:, :, None] * gathered_rows.astype(jnp.float32), axis=1).astype(
        jnp.bfloat16
    )
    mixer_in = rms_rows(
        stream.astype(jnp.float32) + moe_out.astype(jnp.float32), mixer_gain
    ).astype(jnp.bfloat16)
    weight_list = (query_weight, key_weight, value_weight, output_gate, beta_weight, decay_weight)
    piece_rows = lax.all_gather(mixer_in, "head", axis=0, tiled=True)
    projected = jnp.concatenate(
        [jnp.dot(piece_rows, matrix, preferred_element_type=jnp.float32) for matrix in weight_list],
        axis=1,
    )
    row_count = projected.shape[0]
    key_cols = query_weight.shape[1]
    value_cols = value_weight.shape[1]
    head_cols = beta_weight.shape[1]
    conv_cols = 2 * key_cols + value_cols
    qkv_raw = projected[:, :conv_cols].astype(jnp.bfloat16)
    gate_raw = projected[:, conv_cols : conv_cols + value_cols].astype(jnp.bfloat16)
    beta_raw = projected[:, conv_cols + value_cols : conv_cols + value_cols + head_cols]
    decay_raw = projected[:, conv_cols + value_cols + head_cols :]
    taps = jnp.concatenate([query_conv, key_conv, value_conv], axis=1)
    rim_len = taps.shape[0] - 1
    rim_cells = passed_along(qkv_raw[row_count - rim_len :], "ctx", 1)
    extended = jnp.concatenate([rim_cells.astype(jnp.float32), qkv_raw.astype(jnp.float32)], axis=0)
    summed = jnp.zeros((row_count, conv_cols), jnp.float32)
    for shift_index in range(rim_len + 1):
        summed = (
            summed + taps[shift_index][None, :] * extended[shift_index : shift_index + row_count]
        )
    convolved = jax.nn.silu(summed)
    key_width = DK
    key_heads = key_cols // key_width
    group_size = head_cols // key_heads
    queries = unit_heads(convolved[:, :key_cols], key_heads) * key_width ** (-0.5)
    key_rows = unit_heads(convolved[:, key_cols : 2 * key_cols], key_heads)
    values = convolved[:, 2 * key_cols :].reshape(row_count, head_cols, -1)
    strength = jax.nn.sigmoid(beta_raw)
    decays = -jnp.exp(decay_log)[None, :] * jax.nn.softplus(decay_raw + decay_bias[None, :])
    query_heads = jnp.repeat(queries, group_size, axis=1).transpose(1, 0, 2)
    key_head_rows = jnp.repeat(key_rows, group_size, axis=1).transpose(1, 0, 2)
    output_list, read_values, transfer, offset = local_delta(
        query_heads, key_head_rows, values.transpose(1, 0, 2), strength.T, decays.T
    )
    incoming_rows = incoming_state(transfer, offset, "ctx")
    delta_core_output = output_list + jnp.einsum(
        "wnc,wcg->wng", read_values, incoming_rows, precision=exact_precision
    )
    delta_core_output = delta_core_output.transpose(1, 0, 2)
    normal = (
        delta_core_output
        * lax.rsqrt(
            jnp.mean(delta_core_output * delta_core_output, axis=-1, keepdims=True) + epsilon
        )
        * head_gain
    )
    gate_values = gate_raw.astype(jnp.float32).reshape(row_count, head_cols, -1)
    gated_out = (
        (normal * jax.nn.silu(gate_values)).astype(jnp.bfloat16).reshape(row_count, value_cols)
    )
    mixer_out = lax.psum_scatter(
        jnp.dot(gated_out, out_weight, preferred_element_type=jnp.float32).astype(jnp.bfloat16),
        "head",
        scatter_dimension=0,
        tiled=True,
    )
    return (moe_out, mixer_out)


def solution(mesh):
    return jax.shard_map(
        on_device,
        mesh=mesh,
        in_specs=(
            P(("ctx", "head"), None),
            P(),
            P(),
            P(("ctx", "head"), None),
            P(("ctx", "head"), None, None),
            P(("ctx", "head"), None, None),
            P(("ctx", "head"), None, None),
            P(),
            P(None, "head"),
            P(None, "head"),
            P(None, "head"),
            P(None, "head"),
            P(None, "head"),
            P(None, "head"),
            P(None, "head"),
            P(None, "head"),
            P(None, "head"),
            P("head"),
            P("head"),
            P(),
            P("head", None),
        ),
        out_specs=(P(("ctx", "head"), None), P(("ctx", "head"), None)),
        check_vma=False,
    )
```

```python
import math

import jax
import jax.numpy as jnp
from jax import lax
from jax.experimental import pallas as pl
from jax.experimental.pallas import tpu as pltpu
from jax.sharding import PartitionSpec as P

DK = 128
HI = lax.Precision.HIGHEST
CHUNK = 64
UNROLL = 2
epsilon = 1e-06


def _mm(a, b):
    return jnp.dot(a, b, precision=HI, preferred_element_type=jnp.float32)


def _mm_nt(a, b):
    return lax.dot_general(a, b, (((1,), (1,)), ((), ())), precision=HI,
                           preferred_element_type=jnp.float32)


def _mm_tn(a, b):
    return lax.dot_general(a, b, (((0,), (0,)), ((), ())), precision=HI,
                           preferred_element_type=jnp.float32)


def delta_kernel(q_ref, k_ref, v_ref, b_ref, cc_ref, cr_ref, out_ref, carry_ref):
    length, kw = q_ref.shape[1], q_ref.shape[2]
    vw = v_ref.shape[2]
    n_chunks = length // CHUNK
    row = lax.broadcasted_iota(jnp.int32, (CHUNK, CHUNK), 0)
    col = lax.broadcasted_iota(jnp.int32, (CHUNK, CHUNK), 1)
    strict = row > col
    inclusive = row >= col
    eye_c = jnp.where(row == col, 1.0, 0.0).astype(jnp.float32)
    lane = lax.broadcasted_iota(jnp.int32, (CHUNK, vw + kw), 1)
    value_lanes = lane < vw
    krow = lax.broadcasted_iota(jnp.int32, (kw, vw + kw), 0)
    kcol = lax.broadcasted_iota(jnp.int32, (kw, vw + kw), 1)
    carry0 = jnp.where(kcol - vw == krow, 1.0, 0.0).astype(jnp.float32)

    def body(c, carry):
        rows = pl.ds(pl.multiple_of(c * CHUNK, CHUNK), CHUNK)
        q = q_ref[0, rows, :]
        k = k_ref[0, rows, :]
        v = v_ref[0, rows, :]
        beta = b_ref[0, rows, :]
        cum_c = cc_ref[0, rows, :]
        cum_r = cr_ref[0, pl.ds(c, 1), :]
        spread = cum_c - cum_r
        fall_s = jnp.where(strict, jnp.exp(jnp.where(strict, spread, 0.0)), 0.0)
        fall_i = jnp.where(inclusive, jnp.exp(jnp.where(inclusive, spread, 0.0)), 0.0)
        a = beta * fall_s * _mm_nt(k, k)
        inv = eye_c
        size = 1
        while size < CHUNK:
            band = ((row // (2 * size)) == (col // (2 * size))) & ((row // size) != (col // size))
            e = jnp.where(band, a, 0.0)
            inv = inv - _mm(_mm(inv, e), inv)
            size *= 2
        ec = jnp.exp(cum_c)
        solved = _mm(inv, jnp.concatenate([beta * v, (beta * ec) * k], axis=1))
        w_values = jnp.where(value_lanes, solved, 0.0)
        w_keys = solved[:, vw:]
        mixing = fall_i * _mm_nt(q, k)
        q_dec = ec * q
        last = cum_r[:, CHUNK - 1:CHUNK]
        k_dec = jnp.exp(last - cum_c) * k
        closing = jnp.exp(last)
        change = w_values - _mm(w_keys, carry)
        out_ref[0, rows, :] = _mm(q_dec, carry) + _mm(mixing, change)
        return closing * carry + _mm_tn(k_dec, change)

    carry_ref[0] = lax.fori_loop(0, n_chunks, body, carry0, unroll=UNROLL)


def local_delta(queries, key_rows, values, strength, decays):
    heads, length, kw = queries.shape
    vw = values.shape[2]
    n_chunks = length // CHUNK
    cum = jnp.cumsum(decays.reshape(heads, n_chunks, CHUNK), axis=-1)
    cum_col = cum.reshape(heads, length, 1)
    beta_col = strength.reshape(heads, length, 1)
    seq = lambda w: pl.BlockSpec((1, length, w), lambda h: (h, 0, 0))
    out, carry = pl.pallas_call(
        delta_kernel,
        grid=(heads,),
        in_specs=[seq(kw), seq(kw), seq(vw), seq(1), seq(1),
                  pl.BlockSpec((1, n_chunks, CHUNK), lambda h: (h, 0, 0))],
        out_specs=[seq(vw + kw), pl.BlockSpec((1, kw, vw + kw), lambda h: (h, 0, 0))],
        out_shape=[jax.ShapeDtypeStruct((heads, length, vw + kw), jnp.float32),
                   jax.ShapeDtypeStruct((heads, kw, vw + kw), jnp.float32)],
        name="delta_chunks",
    )(queries, key_rows, values, beta_col, cum_col, cum)
    return out, carry


def passed_along(value, axis, steps):
    count = lax.axis_size(axis)
    first, last = (max(0, -steps), min(count, count - steps))
    return lax.ppermute(value, axis, [(source, source + steps) for source in range(first, last)])


def shifted(value, axis, steps):
    count = lax.axis_size(axis)
    return lax.ppermute(value, axis, [(source, source + steps) for source in range(count - steps)])


def batched_mm(a, b):
    return jnp.einsum("hij,hjk->hik", a, b, precision=HI)


def incoming_state(pair, axis):
    count, place = lax.axis_size(axis), lax.axis_index(axis)
    value_width = pair.shape[2] - pair.shape[1]
    offset_lanes = lax.broadcasted_iota(jnp.int32, pair.shape, 2) < value_width
    steps = 1
    while steps < count:
        reached = place >= steps
        transfer = pair[..., value_width:]
        if 2 * steps < count:
            far = shifted(pair, axis, steps)
            joined = batched_mm(transfer, far) + jnp.where(offset_lanes, pair, 0.0)
            pair = jnp.where(reached, joined, pair)
        else:
            far = shifted(pair[..., :value_width], axis, steps)
            offset = pair[..., :value_width]
            offset = jnp.where(reached, offset + batched_mm(transfer, far), offset)
        steps *= 2
    return shifted(offset, axis, 1)


def rms_rows(values, gain):
    values = values.astype(jnp.float32)
    scale = lax.rsqrt(jnp.mean(values * values, axis=-1, keepdims=True) + epsilon)
    return values * scale * gain


def unit_heads(array, heads):
    reshaped_rows = array.reshape(array.shape[0], heads, -1)
    return reshaped_rows * lax.rsqrt(
        jnp.sum(reshaped_rows * reshaped_rows, axis=-1, keepdims=True) + epsilon
    )


def on_device(
    stream,
    moe_gain,
    router,
    expert_ids,
    expert_gate,
    expert_up,
    expert_down,
    mixer_gain,
    query_weight,
    key_weight,
    value_weight,
    output_gate,
    beta_weight,
    decay_weight,
    query_conv,
    key_conv,
    value_conv,
    decay_log,
    decay_bias,
    head_gain,
    out_weight,
):
    ctx_count = lax.axis_size("ctx")
    head_count = lax.axis_size("head")
    sources = ctx_count * head_count
    tok_rows, model_width = stream.shape
    top_count = expert_ids.shape[1]
    local_experts = expert_gate.shape[0]
    experts_all = local_experts * sources
    capacity = (11 * tok_rows * top_count + 10 * experts_all - 1) // (10 * experts_all)
    normed = rms_rows(stream, moe_gain).astype(jnp.bfloat16)
    logits = jnp.dot(normed, router, preferred_element_type=jnp.float32)
    expert_hit = expert_ids[:, :, None] == jnp.arange(experts_all, dtype=jnp.int32)[None, None, :]
    chosen = jnp.sum(jnp.where(expert_hit, logits[:, None, :], 0.0), axis=2)
    raised = jnp.exp(chosen)
    weights = raised / jnp.sum(raised, axis=1, keepdims=True)
    flat_ids = expert_ids.reshape(-1)
    matches = (flat_ids[:, None] == jnp.arange(experts_all, dtype=jnp.int32)[None, :]).astype(
        jnp.int32
    )
    slot_index = jnp.sum((jnp.cumsum(matches, axis=0) - 1) * matches, axis=1)
    places = flat_ids * capacity + slot_index
    slot_count = experts_all * capacity
    place_rows = places.reshape(tok_rows, top_count)
    slot_ids = jnp.arange(slot_count, dtype=jnp.int32)
    take = jnp.sum((place_rows[None, :, :] == slot_ids[:, None, None]).astype(jnp.float32), axis=2)
    outgoing = jnp.dot(
        take.astype(jnp.bfloat16), normed, preferred_element_type=jnp.float32
    ).astype(jnp.bfloat16)
    outgoing = outgoing.reshape(sources, local_experts, capacity, model_width)
    received = lax.all_to_all(outgoing, ("ctx", "head"), split_axis=0, concat_axis=0, tiled=True)
    gate_part = jnp.einsum(
        "nesd,edh->nesh", received, expert_gate, preferred_element_type=jnp.float32
    )
    up_part = jnp.einsum("nesd,edh->nesh", received, expert_up, preferred_element_type=jnp.float32)
    hidden = (jax.nn.silu(gate_part) * up_part).astype(jnp.bfloat16)
    returned = lax.all_to_all(
        jnp.einsum(
            "nesh,ehd->nesd", hidden, expert_down, preferred_element_type=jnp.float32
        ).astype(jnp.bfloat16),
        ("ctx", "head"),
        split_axis=0,
        concat_axis=0,
        tiled=True,
    )
    mix = jnp.sum(
        jnp.where(place_rows[:, :, None] == slot_ids[None, None, :], weights[:, :, None], 0.0), axis=1
    )
    moe_out = jnp.dot(
        mix, returned.reshape(slot_count, model_width).astype(jnp.float32), precision=HI
    ).astype(jnp.bfloat16)
    mixer_in = rms_rows(
        stream.astype(jnp.float32) + moe_out.astype(jnp.float32), mixer_gain
    ).astype(jnp.bfloat16)
    weight_list = (query_weight, key_weight, value_weight, output_gate, beta_weight, decay_weight)
    piece_rows = lax.all_gather(mixer_in, "head", axis=0, tiled=True)
    projected = jnp.concatenate(
        [jnp.dot(piece_rows, matrix, preferred_element_type=jnp.float32) for matrix in weight_list],
        axis=1,
    )
    row_count = projected.shape[0]
    key_cols = query_weight.shape[1]
    value_cols = value_weight.shape[1]
    head_cols = beta_weight.shape[1]
    conv_cols = 2 * key_cols + value_cols
    qkv_raw = projected[:, :conv_cols].astype(jnp.bfloat16)
    gate_raw = projected[:, conv_cols : conv_cols + value_cols].astype(jnp.bfloat16)
    beta_raw = projected[:, conv_cols + value_cols : conv_cols + value_cols + head_cols]
    decay_raw = projected[:, conv_cols + value_cols + head_cols :]
    taps = jnp.concatenate([query_conv, key_conv, value_conv], axis=1)
    rim_len = taps.shape[0] - 1
    rim_cells = passed_along(qkv_raw[row_count - rim_len :], "ctx", 1)
    extended = jnp.concatenate([rim_cells.astype(jnp.float32), qkv_raw.astype(jnp.float32)], axis=0)
    summed = jnp.zeros((row_count, conv_cols), jnp.float32)
    for shift_index in range(rim_len + 1):
        summed = (
            summed + taps[shift_index][None, :] * extended[shift_index : shift_index + row_count]
        )
    convolved = jax.nn.silu(summed)
    key_width = DK
    key_heads = key_cols // key_width
    group_size = head_cols // key_heads
    queries = unit_heads(convolved[:, :key_cols], key_heads) * key_width ** (-0.5)
    key_rows = unit_heads(convolved[:, key_cols : 2 * key_cols], key_heads)
    values = convolved[:, 2 * key_cols :].reshape(row_count, head_cols, -1)
    strength = jax.nn.sigmoid(beta_raw)
    decays = -jnp.exp(decay_log)[None, :] * jax.nn.softplus(decay_raw + decay_bias[None, :])
    query_heads = jnp.repeat(queries, group_size, axis=1).transpose(1, 0, 2)
    key_head_rows = jnp.repeat(key_rows, group_size, axis=1).transpose(1, 0, 2)
    core_parts, carry = local_delta(
        query_heads, key_head_rows, values.transpose(1, 0, 2), strength.T, decays.T
    )
    incoming_rows = incoming_state(carry, "ctx")
    value_width = values.shape[2]
    delta_core_output = core_parts[..., :value_width] + jnp.einsum(
        "wnc,wcg->wng", core_parts[..., value_width:], incoming_rows, precision=HI
    )
    delta_core_output = delta_core_output.transpose(1, 0, 2)
    normal = (
        delta_core_output
        * lax.rsqrt(
            jnp.mean(delta_core_output * delta_core_output, axis=-1, keepdims=True) + epsilon
        )
        * head_gain
    )
    gate_values = gate_raw.astype(jnp.float32).reshape(row_count, head_cols, -1)
    gated_out = (
        (normal * jax.nn.silu(gate_values)).astype(jnp.bfloat16).reshape(row_count, value_cols)
    )
    mixer_out = lax.psum_scatter(
        jnp.dot(gated_out, out_weight, preferred_element_type=jnp.float32).astype(jnp.bfloat16),
        "head",
        scatter_dimension=0,
        tiled=True,
    )
    return (moe_out, mixer_out)


def solution(mesh):
    return jax.shard_map(
        on_device,
        mesh=mesh,
        in_specs=(
            P(("ctx", "head"), None),
            P(),
            P(),
            P(("ctx", "head"), None),
            P(("ctx", "head"), None, None),
            P(("ctx", "head"), None, None),
            P(("ctx", "head"), None, None),
            P(),
            P(None, "head"),
            P(None, "head"),
            P(None, "head"),
            P(None, "head"),
            P(None, "head"),
            P(None, "head"),
            P(None, "head"),
            P(None, "head"),
            P(None, "head"),
            P("head"),
            P("head"),
            P(),
            P("head", None),
        ),
        out_specs=(P(("ctx", "head"), None), P(("ctx", "head"), None)),
        check_vma=False,
    )
```

```python
import math

import jax
import jax.numpy as jnp
from jax import lax
from jax.experimental import pallas as pl
from jax.experimental.pallas import tpu as pltpu
from jax.sharding import PartitionSpec as P

DK = 128
HI = lax.Precision.HIGHEST
CHUNK = 64
epsilon = 1e-06


def _mm(a, b):
    return jnp.dot(a, b, precision=HI, preferred_element_type=jnp.float32)


def _mm_nt(a, b):
    return lax.dot_general(a, b, (((1,), (1,)), ((), ())), precision=HI,
                           preferred_element_type=jnp.float32)


def _mm_tn(a, b):
    return lax.dot_general(a, b, (((0,), (0,)), ((), ())), precision=HI,
                           preferred_element_type=jnp.float32)


def delta_kernel(q_ref, k_ref, v_ref, b_ref, cc_ref, cr_ref, out_ref, carry_ref):
    heads, length, kw = q_ref.shape
    vw = v_ref.shape[2]
    n_chunks = length // CHUNK
    row = lax.broadcasted_iota(jnp.int32, (CHUNK, CHUNK), 0)
    col = lax.broadcasted_iota(jnp.int32, (CHUNK, CHUNK), 1)
    strict = row > col
    inclusive = row >= col
    eye_c = jnp.where(row == col, 1.0, 0.0).astype(jnp.float32)
    pairs = ((row // 2) == (col // 2)) & (row != col)
    lane = lax.broadcasted_iota(jnp.int32, (CHUNK, vw + kw), 1)
    value_lanes = lane < vw
    krow = lax.broadcasted_iota(jnp.int32, (kw, vw + kw), 0)
    kcol = lax.broadcasted_iota(jnp.int32, (kw, vw + kw), 1)
    carry0 = jnp.where(kcol - vw == krow, 1.0, 0.0).astype(jnp.float32)

    def one_head(h, c, carry):
        rows = pl.ds(pl.multiple_of(c * CHUNK, CHUNK), CHUNK)
        q = q_ref[h, rows, :]
        k = k_ref[h, rows, :]
        v = v_ref[h, rows, :]
        beta = b_ref[h, rows, :]
        cum_c = cc_ref[h, rows, :]
        cum_r = cr_ref[h, pl.ds(c, 1), :]
        spread = cum_c - cum_r
        fall_s = jnp.where(strict, jnp.exp(jnp.where(strict, spread, 0.0)), 0.0)
        fall_i = jnp.where(inclusive, jnp.exp(jnp.where(inclusive, spread, 0.0)), 0.0)
        a = beta * fall_s * _mm_nt(k, k)
        inv = eye_c - jnp.where(pairs, a, 0.0)
        size = 2
        while size < CHUNK:
            band = ((row // (2 * size)) == (col // (2 * size))) & ((row // size) != (col // size))
            e = jnp.where(band, a, 0.0)
            inv = inv - _mm(_mm(inv, e), inv)
            size *= 2
        ec = jnp.exp(cum_c)
        solved = _mm(inv, jnp.concatenate([beta * v, (beta * ec) * k], axis=1))
        w_values = jnp.where(value_lanes, solved, 0.0)
        w_keys = solved[:, vw:]
        mixing = fall_i * _mm_nt(q, k)
        q_dec = ec * q
        last = cum_r[:, CHUNK - 1:CHUNK]
        k_dec = jnp.exp(last - cum_c) * k
        closing = jnp.exp(last)
        change = w_values - _mm(w_keys, carry)
        out_ref[h, rows, :] = _mm(q_dec, carry) + _mm(mixing, change)
        return closing * carry + _mm_tn(k_dec, change)

    def body(c, carries):
        return tuple(one_head(h, c, carries[h]) for h in range(heads))

    carries = lax.fori_loop(0, n_chunks, body, (carry0,) * heads)
    for h in range(heads):
        carry_ref[h] = carries[h]


def local_delta(queries, key_rows, values, strength, decays):
    heads, length, kw = queries.shape
    vw = values.shape[2]
    n_chunks = length // CHUNK
    cum = jnp.cumsum(decays.reshape(heads, n_chunks, CHUNK), axis=-1)
    cum_col = cum.reshape(heads, length, 1)
    beta_col = strength.reshape(heads, length, 1)
    whole = lambda *shape: pl.BlockSpec(shape, lambda i: (0,) * len(shape))
    return pl.pallas_call(
        delta_kernel,
        grid=(1,),
        in_specs=[whole(heads, length, kw), whole(heads, length, kw), whole(heads, length, vw),
                  whole(heads, length, 1), whole(heads, length, 1), whole(heads, n_chunks, CHUNK)],
        out_specs=[whole(heads, length, vw + kw), whole(heads, kw, vw + kw)],
        out_shape=[jax.ShapeDtypeStruct((heads, length, vw + kw), jnp.float32),
                   jax.ShapeDtypeStruct((heads, kw, vw + kw), jnp.float32)],
        name="delta_chunks",
    )(queries, key_rows, values, beta_col, cum_col, cum)


def passed_along(value, axis, steps):
    count = lax.axis_size(axis)
    first, last = (max(0, -steps), min(count, count - steps))
    return lax.ppermute(value, axis, [(source, source + steps) for source in range(first, last)])


def shifted(value, axis, steps):
    count = lax.axis_size(axis)
    return lax.ppermute(value, axis, [(source, source + steps) for source in range(count - steps)])


def batched_mm(a, b):
    return jnp.einsum("hij,hjk->hik", a, b, precision=HI)


def incoming_state(pair, axis):
    count, place = lax.axis_size(axis), lax.axis_index(axis)
    value_width = pair.shape[2] - pair.shape[1]
    offset_lanes = lax.broadcasted_iota(jnp.int32, pair.shape, 2) < value_width
    steps = 1
    while steps < count:
        reached = place >= steps
        transfer = pair[..., value_width:]
        if 2 * steps < count:
            far = shifted(pair, axis, steps)
            joined = batched_mm(transfer, far) + jnp.where(offset_lanes, pair, 0.0)
            pair = jnp.where(reached, joined, pair)
        else:
            far = shifted(pair[..., :value_width], axis, steps)
            offset = pair[..., :value_width]
            offset = jnp.where(reached, offset + batched_mm(transfer, far), offset)
        steps *= 2
    return shifted(offset, axis, 1)


def rms_rows(values, gain):
    values = values.astype(jnp.float32)
    scale = lax.rsqrt(jnp.mean(values * values, axis=-1, keepdims=True) + epsilon)
    return values * scale * gain


def unit_heads(array, heads):
    reshaped_rows = array.reshape(array.shape[0], heads, -1)
    return reshaped_rows * lax.rsqrt(
        jnp.sum(reshaped_rows * reshaped_rows, axis=-1, keepdims=True) + epsilon
    )


def on_device(
    stream,
    moe_gain,
    router,
    expert_ids,
    expert_gate,
    expert_up,
    expert_down,
    mixer_gain,
    query_weight,
    key_weight,
    value_weight,
    output_gate,
    beta_weight,
    decay_weight,
    query_conv,
    key_conv,
    value_conv,
    decay_log,
    decay_bias,
    head_gain,
    out_weight,
):
    ctx_count = lax.axis_size("ctx")
    head_count = lax.axis_size("head")
    sources = ctx_count * head_count
    tok_rows, model_width = stream.shape
    top_count = expert_ids.shape[1]
    local_experts = expert_gate.shape[0]
    experts_all = local_experts * sources
    capacity = (11 * tok_rows * top_count + 10 * experts_all - 1) // (10 * experts_all)
    normed = rms_rows(stream, moe_gain).astype(jnp.bfloat16)
    logits = jnp.dot(normed, router, preferred_element_type=jnp.float32)
    expert_hit = expert_ids[:, :, None] == jnp.arange(experts_all, dtype=jnp.int32)[None, None, :]
    chosen = jnp.sum(jnp.where(expert_hit, logits[:, None, :], 0.0), axis=2)
    raised = jnp.exp(chosen)
    weights = raised / jnp.sum(raised, axis=1, keepdims=True)
    flat_ids = expert_ids.reshape(-1)
    matches = (flat_ids[:, None] == jnp.arange(experts_all, dtype=jnp.int32)[None, :]).astype(
        jnp.int32
    )
    slot_index = jnp.sum((jnp.cumsum(matches, axis=0) - 1) * matches, axis=1)
    places = flat_ids * capacity + slot_index
    slot_count = experts_all * capacity
    place_rows = places.reshape(tok_rows, top_count)
    slot_ids = jnp.arange(slot_count, dtype=jnp.int32)
    take = jnp.sum((place_rows[None, :, :] == slot_ids[:, None, None]).astype(jnp.float32), axis=2)
    outgoing = jnp.dot(
        take.astype(jnp.bfloat16), normed, preferred_element_type=jnp.float32
    ).astype(jnp.bfloat16)
    outgoing = outgoing.reshape(sources, local_experts, capacity, model_width)
    received = lax.all_to_all(outgoing, ("ctx", "head"), split_axis=0, concat_axis=0, tiled=True)
    gate_part = jnp.einsum(
        "nesd,edh->nesh", received, expert_gate, preferred_element_type=jnp.float32
    )
    up_part = jnp.einsum("nesd,edh->nesh", received, expert_up, preferred_element_type=jnp.float32)
    hidden = (jax.nn.silu(gate_part) * up_part).astype(jnp.bfloat16)
    returned = lax.all_to_all(
        jnp.einsum(
            "nesh,ehd->nesd", hidden, expert_down, preferred_element_type=jnp.float32
        ).astype(jnp.bfloat16),
        ("ctx", "head"),
        split_axis=0,
        concat_axis=0,
        tiled=True,
    )
    mix = jnp.sum(
        jnp.where(place_rows[:, :, None] == slot_ids[None, None, :], weights[:, :, None], 0.0), axis=1
    )
    moe_out = jnp.dot(
        mix, returned.reshape(slot_count, model_width).astype(jnp.float32), precision=HI
    ).astype(jnp.bfloat16)
    mixer_in = rms_rows(
        stream.astype(jnp.float32) + moe_out.astype(jnp.float32), mixer_gain
    ).astype(jnp.bfloat16)
    weight_list = (query_weight, key_weight, value_weight, output_gate, beta_weight, decay_weight)
    piece_rows = lax.all_gather(mixer_in, "head", axis=0, tiled=True)
    projected = jnp.concatenate(
        [jnp.dot(piece_rows, matrix, preferred_element_type=jnp.float32) for matrix in weight_list],
        axis=1,
    )
    row_count = projected.shape[0]
    key_cols = query_weight.shape[1]
    value_cols = value_weight.shape[1]
    head_cols = beta_weight.shape[1]
    conv_cols = 2 * key_cols + value_cols
    qkv_raw = projected[:, :conv_cols].astype(jnp.bfloat16)
    gate_raw = projected[:, conv_cols : conv_cols + value_cols].astype(jnp.bfloat16)
    beta_raw = projected[:, conv_cols + value_cols : conv_cols + value_cols + head_cols]
    decay_raw = projected[:, conv_cols + value_cols + head_cols :]
    taps = jnp.concatenate([query_conv, key_conv, value_conv], axis=1)
    rim_len = taps.shape[0] - 1
    rim_cells = passed_along(qkv_raw[row_count - rim_len :], "ctx", 1)
    extended = jnp.concatenate([rim_cells.astype(jnp.float32), qkv_raw.astype(jnp.float32)], axis=0)
    summed = jnp.zeros((row_count, conv_cols), jnp.float32)
    for shift_index in range(rim_len + 1):
        summed = (
            summed + taps[shift_index][None, :] * extended[shift_index : shift_index + row_count]
        )
    convolved = jax.nn.silu(summed)
    key_width = DK
    key_heads = key_cols // key_width
    group_size = head_cols // key_heads
    queries = unit_heads(convolved[:, :key_cols], key_heads) * key_width ** (-0.5)
    key_rows = unit_heads(convolved[:, key_cols : 2 * key_cols], key_heads)
    values = convolved[:, 2 * key_cols :].reshape(row_count, head_cols, -1)
    strength = jax.nn.sigmoid(beta_raw)
    decays = -jnp.exp(decay_log)[None, :] * jax.nn.softplus(decay_raw + decay_bias[None, :])
    query_heads = jnp.repeat(queries, group_size, axis=1).transpose(1, 0, 2)
    key_head_rows = jnp.repeat(key_rows, group_size, axis=1).transpose(1, 0, 2)
    core_parts, carry = local_delta(
        query_heads, key_head_rows, values.transpose(1, 0, 2), strength.T, decays.T
    )
    incoming_rows = incoming_state(carry, "ctx")
    value_width = values.shape[2]
    delta_core_output = core_parts[..., :value_width] + jnp.einsum(
        "wnc,wcg->wng", core_parts[..., value_width:], incoming_rows, precision=HI
    )
    delta_core_output = delta_core_output.transpose(1, 0, 2)
    normal = (
        delta_core_output
        * lax.rsqrt(
            jnp.mean(delta_core_output * delta_core_output, axis=-1, keepdims=True) + epsilon
        )
        * head_gain
    )
    gate_values = gate_raw.astype(jnp.float32).reshape(row_count, head_cols, -1)
    gated_out = (
        (normal * jax.nn.silu(gate_values)).astype(jnp.bfloat16).reshape(row_count, value_cols)
    )
    mixer_out = lax.psum_scatter(
        jnp.dot(gated_out, out_weight, preferred_element_type=jnp.float32).astype(jnp.bfloat16),
        "head",
        scatter_dimension=0,
        tiled=True,
    )
    return (moe_out, mixer_out)


def solution(mesh):
    return jax.shard_map(
        on_device,
        mesh=mesh,
        in_specs=(
            P(("ctx", "head"), None),
            P(),
            P(),
            P(("ctx", "head"), None),
            P(("ctx", "head"), None, None),
            P(("ctx", "head"), None, None),
            P(("ctx", "head"), None, None),
            P(),
            P(None, "head"),
            P(None, "head"),
            P(None, "head"),
            P(None, "head"),
            P(None, "head"),
            P(None, "head"),
            P(None, "head"),
            P(None, "head"),
            P(None, "head"),
            P("head"),
            P("head"),
            P(),
            P("head", None),
        ),
        out_specs=(P(("ctx", "head"), None), P(("ctx", "head"), None)),
        check_vma=False,
    )
```

```python
import math

import jax
import jax.numpy as jnp
from jax import lax
from jax.experimental import pallas as pl
from jax.experimental.pallas import tpu as pltpu
from jax.sharding import PartitionSpec as P

DK = 128
HI = lax.Precision.HIGHEST
CHUNK = 64
epsilon = 1e-06


def _mm(a, b):
    return jnp.dot(a, b, precision=HI, preferred_element_type=jnp.float32)


def _mm_nt(a, b):
    return lax.dot_general(a, b, (((1,), (1,)), ((), ())), precision=HI,
                           preferred_element_type=jnp.float32)


def _mm_tn(a, b):
    return lax.dot_general(a, b, (((0,), (0,)), ((), ())), precision=HI,
                           preferred_element_type=jnp.float32)


def delta_kernel(q_ref, k_ref, v_ref, b_ref, cc_ref, cr_ref, out_ref, carry_ref):
    heads, length, kw = q_ref.shape
    vw = v_ref.shape[2]
    n_chunks = length // CHUNK
    row = lax.broadcasted_iota(jnp.int32, (CHUNK, CHUNK), 0)
    col = lax.broadcasted_iota(jnp.int32, (CHUNK, CHUNK), 1)
    strict = row > col
    inclusive = row >= col
    eye_c = jnp.where(row == col, 1.0, 0.0).astype(jnp.float32)
    pairs = ((row // 2) == (col // 2)) & (row != col)
    lane = lax.broadcasted_iota(jnp.int32, (CHUNK, vw + kw), 1)
    value_lanes = lane < vw
    krow = lax.broadcasted_iota(jnp.int32, (kw, vw + kw), 0)
    kcol = lax.broadcasted_iota(jnp.int32, (kw, vw + kw), 1)
    carry0 = jnp.where(kcol - vw == krow, 1.0, 0.0).astype(jnp.float32)

    def one_head(h, c, carry):
        rows = pl.ds(pl.multiple_of(c * CHUNK, CHUNK), CHUNK)
        q = q_ref[h, rows, :]
        k = k_ref[h, rows, :]
        v = v_ref[h, rows, :]
        beta = b_ref[h, rows, :]
        cum_c = cc_ref[h, rows, :]
        cum_r = cr_ref[h, pl.ds(c, 1), :]
        spread = cum_c - cum_r
        fall_s = jnp.where(strict, jnp.exp(jnp.where(strict, spread, 0.0)), 0.0)
        fall_i = jnp.where(inclusive, jnp.exp(jnp.where(inclusive, spread, 0.0)), 0.0)
        a = beta * fall_s * _mm_nt(k, k)
        inv = eye_c - jnp.where(pairs, a, 0.0)
        size = 2
        while size < CHUNK:
            band = ((row // (2 * size)) == (col // (2 * size))) & ((row // size) != (col // size))
            e = jnp.where(band, a, 0.0)
            inv = inv - _mm(_mm(inv, e), inv)
            size *= 2
        ec = jnp.exp(cum_c)
        solved = _mm(inv, jnp.concatenate([beta * v, (beta * ec) * k], axis=1))
        w_values = jnp.where(value_lanes, solved, 0.0)
        w_keys = solved[:, vw:]
        mixing = fall_i * _mm_nt(q, k)
        q_dec = ec * q
        last = cum_r[:, CHUNK - 1:CHUNK]
        k_dec = jnp.exp(last - cum_c) * k
        closing = jnp.exp(last)
        change = w_values - _mm(w_keys, carry)
        out_ref[h, rows, :] = _mm(q_dec, carry) + _mm(mixing, change)
        return closing * carry + _mm_tn(k_dec, change)

    def body(c, carries):
        return tuple(one_head(h, c, carries[h]) for h in range(heads))

    carries = lax.fori_loop(0, n_chunks, body, (carry0,) * heads)
    for h in range(heads):
        carry_ref[h] = carries[h]


def local_delta(queries, key_rows, values, strength, decays):
    heads, length, kw = queries.shape
    vw = values.shape[2]
    n_chunks = length // CHUNK
    cum = jnp.cumsum(decays.reshape(heads, n_chunks, CHUNK), axis=-1)
    cum_col = cum.reshape(heads, length, 1)
    beta_col = strength.reshape(heads, length, 1)
    whole = lambda *shape: pl.BlockSpec(shape, lambda i: (0,) * len(shape))
    return pl.pallas_call(
        delta_kernel,
        grid=(1,),
        in_specs=[whole(heads, length, kw), whole(heads, length, kw), whole(heads, length, vw),
                  whole(heads, length, 1), whole(heads, length, 1), whole(heads, n_chunks, CHUNK)],
        out_specs=[whole(heads, length, vw + kw), whole(heads, kw, vw + kw)],
        out_shape=[jax.ShapeDtypeStruct((heads, length, vw + kw), jnp.float32),
                   jax.ShapeDtypeStruct((heads, kw, vw + kw), jnp.float32)],
        name="delta_chunks",
    )(queries, key_rows, values, beta_col, cum_col, cum)


def passed_along(value, axis, steps):
    count = lax.axis_size(axis)
    first, last = (max(0, -steps), min(count, count - steps))
    return lax.ppermute(value, axis, [(source, source + steps) for source in range(first, last)])


def shifted(value, axis, steps):
    count = lax.axis_size(axis)
    return lax.ppermute(value, axis, [(source, source + steps) for source in range(count - steps)])


def batched_mm(a, b):
    return jnp.einsum("hij,hjk->hik", a, b, precision=HI)


def incoming_state(pair, axis):
    count, place = lax.axis_size(axis), lax.axis_index(axis)
    value_width = pair.shape[2] - pair.shape[1]
    offset_lanes = lax.broadcasted_iota(jnp.int32, pair.shape, 2) < value_width
    steps = 1
    while steps < count:
        reached = place >= steps
        transfer = pair[..., value_width:]
        if 2 * steps < count:
            far = shifted(pair, axis, steps)
            joined = batched_mm(transfer, far) + jnp.where(offset_lanes, pair, 0.0)
            pair = jnp.where(reached, joined, pair)
        else:
            far = shifted(pair[..., :value_width], axis, steps)
            offset = pair[..., :value_width]
            offset = jnp.where(reached, offset + batched_mm(transfer, far), offset)
        steps *= 2
    return shifted(offset, axis, 1)


def rms_rows(values, gain):
    values = values.astype(jnp.float32)
    scale = lax.rsqrt(jnp.mean(values * values, axis=-1, keepdims=True) + epsilon)
    return values * scale * gain


def unit_heads(array, heads):
    reshaped_rows = array.reshape(array.shape[0], heads, -1)
    return reshaped_rows * lax.rsqrt(
        jnp.sum(reshaped_rows * reshaped_rows, axis=-1, keepdims=True) + epsilon
    )


def on_device(
    stream,
    moe_gain,
    router,
    expert_ids,
    expert_gate,
    expert_up,
    expert_down,
    mixer_gain,
    query_weight,
    key_weight,
    value_weight,
    output_gate,
    beta_weight,
    decay_weight,
    query_conv,
    key_conv,
    value_conv,
    decay_log,
    decay_bias,
    head_gain,
    out_weight,
):
    ctx_count = lax.axis_size("ctx")
    head_count = lax.axis_size("head")
    sources = ctx_count * head_count
    tok_rows, model_width = stream.shape
    top_count = expert_ids.shape[1]
    local_experts = expert_gate.shape[0]
    experts_all = local_experts * sources
    capacity = (11 * tok_rows * top_count + 10 * experts_all - 1) // (10 * experts_all)
    normed = rms_rows(stream, moe_gain).astype(jnp.bfloat16)
    logits = jnp.dot(normed, router, preferred_element_type=jnp.float32)
    expert_hit = expert_ids[:, :, None] == jnp.arange(experts_all, dtype=jnp.int32)[None, None, :]
    chosen = jnp.sum(jnp.where(expert_hit, logits[:, None, :], 0.0), axis=2)
    raised = jnp.exp(chosen)
    weights = raised / jnp.sum(raised, axis=1, keepdims=True)
    flat_ids = expert_ids.reshape(-1)
    matches = (flat_ids[:, None] == jnp.arange(experts_all, dtype=jnp.int32)[None, :]).astype(
        jnp.int32
    )
    slot_index = jnp.sum((jnp.cumsum(matches, axis=0) - 1) * matches, axis=1)
    places = flat_ids * capacity + slot_index
    slot_count = experts_all * capacity
    place_rows = places.reshape(tok_rows, top_count)
    slot_ids = jnp.arange(slot_count, dtype=jnp.int32)
    take = jnp.sum((place_rows[None, :, :] == slot_ids[:, None, None]).astype(jnp.float32), axis=2)
    take = take.astype(jnp.bfloat16).reshape(sources, local_experts, capacity, tok_rows)
    outgoing = jnp.einsum(
        "nest,td->nesd", take, normed, preferred_element_type=jnp.float32
    ).astype(jnp.bfloat16)
    received = lax.all_to_all(outgoing, ("ctx", "head"), split_axis=0, concat_axis=0, tiled=True)
    gate_part = jnp.einsum(
        "nesd,edh->nesh", received, expert_gate, preferred_element_type=jnp.float32
    )
    up_part = jnp.einsum("nesd,edh->nesh", received, expert_up, preferred_element_type=jnp.float32)
    hidden = (jax.nn.silu(gate_part) * up_part).astype(jnp.bfloat16)
    returned = lax.all_to_all(
        jnp.einsum(
            "nesh,ehd->nesd", hidden, expert_down, preferred_element_type=jnp.float32
        ).astype(jnp.bfloat16),
        ("ctx", "head"),
        split_axis=0,
        concat_axis=0,
        tiled=True,
    )
    mix = jnp.sum(
        jnp.where(place_rows[:, :, None] == slot_ids[None, None, :], weights[:, :, None], 0.0), axis=1
    )
    mix = mix.reshape(tok_rows, sources, local_experts, capacity)
    moe_out = jnp.einsum(
        "tnes,nesd->td", mix, returned.astype(jnp.float32), precision=HI
    ).astype(jnp.bfloat16)
    mixer_in = rms_rows(
        stream.astype(jnp.float32) + moe_out.astype(jnp.float32), mixer_gain
    ).astype(jnp.bfloat16)
    weight_list = (query_weight, key_weight, value_weight, output_gate, beta_weight, decay_weight)
    piece_rows = lax.all_gather(mixer_in, "head", axis=0, tiled=True)
    projected = jnp.concatenate(
        [jnp.dot(piece_rows, matrix, preferred_element_type=jnp.float32) for matrix in weight_list],
        axis=1,
    )
    row_count = projected.shape[0]
    key_cols = query_weight.shape[1]
    value_cols = value_weight.shape[1]
    head_cols = beta_weight.shape[1]
    conv_cols = 2 * key_cols + value_cols
    qkv_raw = projected[:, :conv_cols].astype(jnp.bfloat16)
    gate_raw = projected[:, conv_cols : conv_cols + value_cols].astype(jnp.bfloat16)
    beta_raw = projected[:, conv_cols + value_cols : conv_cols + value_cols + head_cols]
    decay_raw = projected[:, conv_cols + value_cols + head_cols :]
    taps = jnp.concatenate([query_conv, key_conv, value_conv], axis=1)
    rim_len = taps.shape[0] - 1
    rim_cells = passed_along(qkv_raw[row_count - rim_len :], "ctx", 1)
    extended = jnp.concatenate([rim_cells.astype(jnp.float32), qkv_raw.astype(jnp.float32)], axis=0)
    summed = jnp.zeros((row_count, conv_cols), jnp.float32)
    for shift_index in range(rim_len + 1):
        summed = (
            summed + taps[shift_index][None, :] * extended[shift_index : shift_index + row_count]
        )
    convolved = jax.nn.silu(summed)
    key_width = DK
    key_heads = key_cols // key_width
    group_size = head_cols // key_heads
    queries = unit_heads(convolved[:, :key_cols], key_heads) * key_width ** (-0.5)
    key_rows = unit_heads(convolved[:, key_cols : 2 * key_cols], key_heads)
    values = convolved[:, 2 * key_cols :].reshape(row_count, head_cols, -1)
    strength = jax.nn.sigmoid(beta_raw)
    decays = -jnp.exp(decay_log)[None, :] * jax.nn.softplus(decay_raw + decay_bias[None, :])
    query_heads = jnp.repeat(queries, group_size, axis=1).transpose(1, 0, 2)
    key_head_rows = jnp.repeat(key_rows, group_size, axis=1).transpose(1, 0, 2)
    core_parts, carry = local_delta(
        query_heads, key_head_rows, values.transpose(1, 0, 2), strength.T, decays.T
    )
    incoming_rows = incoming_state(carry, "ctx")
    value_width = values.shape[2]
    delta_core_output = core_parts[..., :value_width] + jnp.einsum(
        "wnc,wcg->wng", core_parts[..., value_width:], incoming_rows, precision=HI
    )
    delta_core_output = delta_core_output.transpose(1, 0, 2)
    normal = (
        delta_core_output
        * lax.rsqrt(
            jnp.mean(delta_core_output * delta_core_output, axis=-1, keepdims=True) + epsilon
        )
        * head_gain
    )
    gate_values = gate_raw.astype(jnp.float32).reshape(row_count, head_cols, -1)
    gated_out = (
        (normal * jax.nn.silu(gate_values)).astype(jnp.bfloat16).reshape(row_count, value_cols)
    )
    mixer_out = lax.psum_scatter(
        jnp.dot(gated_out, out_weight, preferred_element_type=jnp.float32).astype(jnp.bfloat16),
        "head",
        scatter_dimension=0,
        tiled=True,
    )
    return (moe_out, mixer_out)


def solution(mesh):
    return jax.shard_map(
        on_device,
        mesh=mesh,
        in_specs=(
            P(("ctx", "head"), None),
            P(),
            P(),
            P(("ctx", "head"), None),
            P(("ctx", "head"), None, None),
            P(("ctx", "head"), None, None),
            P(("ctx", "head"), None, None),
            P(),
            P(None, "head"),
            P(None, "head"),
            P(None, "head"),
            P(None, "head"),
            P(None, "head"),
            P(None, "head"),
            P(None, "head"),
            P(None, "head"),
            P(None, "head"),
            P("head"),
            P("head"),
            P(),
            P("head", None),
        ),
        out_specs=(P(("ctx", "head"), None), P(("ctx", "head"), None)),
        check_vma=False,
    )
```

```python
import math

import jax
import jax.numpy as jnp
from jax import lax
from jax.experimental import pallas as pl
from jax.experimental.pallas import tpu as pltpu
from jax.sharding import PartitionSpec as P

DK = 128
HI = lax.Precision.HIGHEST
KERNEL_PRECISION = lax.Precision.HIGH
CHUNK = 64
epsilon = 1e-06


def _mm(a, b):
    return jnp.dot(a, b, precision=KERNEL_PRECISION, preferred_element_type=jnp.float32)


def _mm_nt(a, b):
    return lax.dot_general(a, b, (((1,), (1,)), ((), ())), precision=KERNEL_PRECISION,
                           preferred_element_type=jnp.float32)


def _mm_tn(a, b):
    return lax.dot_general(a, b, (((0,), (0,)), ((), ())), precision=KERNEL_PRECISION,
                           preferred_element_type=jnp.float32)


def delta_kernel(q_ref, k_ref, v_ref, b_ref, cc_ref, cr_ref, out_ref, carry_ref):
    heads, length, kw = q_ref.shape
    vw = v_ref.shape[2]
    n_chunks = length // CHUNK
    row = lax.broadcasted_iota(jnp.int32, (CHUNK, CHUNK), 0)
    col = lax.broadcasted_iota(jnp.int32, (CHUNK, CHUNK), 1)
    strict = row > col
    inclusive = row >= col
    eye_c = jnp.where(row == col, 1.0, 0.0).astype(jnp.float32)
    pairs = ((row // 2) == (col // 2)) & (row != col)
    lane = lax.broadcasted_iota(jnp.int32, (CHUNK, vw + kw), 1)
    value_lanes = lane < vw
    krow = lax.broadcasted_iota(jnp.int32, (kw, vw + kw), 0)
    kcol = lax.broadcasted_iota(jnp.int32, (kw, vw + kw), 1)
    carry0 = jnp.where(kcol - vw == krow, 1.0, 0.0).astype(jnp.float32)

    def one_head(h, c, carry):
        rows = pl.ds(pl.multiple_of(c * CHUNK, CHUNK), CHUNK)
        q = q_ref[h, rows, :]
        k = k_ref[h, rows, :]
        v = v_ref[h, rows, :]
        beta = b_ref[h, rows, :]
        cum_c = cc_ref[h, rows, :]
        cum_r = cr_ref[h, pl.ds(c, 1), :]
        spread = cum_c - cum_r
        fall_s = jnp.where(strict, jnp.exp(jnp.where(strict, spread, 0.0)), 0.0)
        fall_i = jnp.where(inclusive, jnp.exp(jnp.where(inclusive, spread, 0.0)), 0.0)
        a = beta * fall_s * _mm_nt(k, k)
        inv = eye_c - jnp.where(pairs, a, 0.0)
        size = 2
        while size < CHUNK:
            band = ((row // (2 * size)) == (col // (2 * size))) & ((row // size) != (col // size))
            e = jnp.where(band, a, 0.0)
            inv = inv - _mm(_mm(inv, e), inv)
            size *= 2
        ec = jnp.exp(cum_c)
        solved = _mm(inv, jnp.concatenate([beta * v, (beta * ec) * k], axis=1))
        w_values = jnp.where(value_lanes, solved, 0.0)
        w_keys = solved[:, vw:]
        mixing = fall_i * _mm_nt(q, k)
        q_dec = ec * q
        last = cum_r[:, CHUNK - 1:CHUNK]
        k_dec = jnp.exp(last - cum_c) * k
        closing = jnp.exp(last)
        change = w_values - _mm(w_keys, carry)
        out_ref[h, rows, :] = _mm(q_dec, carry) + _mm(mixing, change)
        return closing * carry + _mm_tn(k_dec, change)

    def body(c, carries):
        return tuple(one_head(h, c, carries[h]) for h in range(heads))

    carries = lax.fori_loop(0, n_chunks, body, (carry0,) * heads)
    for h in range(heads):
        carry_ref[h] = carries[h]


def local_delta(queries, key_rows, values, strength, decays):
    heads, length, kw = queries.shape
    vw = values.shape[2]
    n_chunks = length // CHUNK
    cum = jnp.cumsum(decays.reshape(heads, n_chunks, CHUNK), axis=-1)
    cum_col = cum.reshape(heads, length, 1)
    beta_col = strength.reshape(heads, length, 1)
    whole = lambda *shape: pl.BlockSpec(shape, lambda i: (0,) * len(shape))
    return pl.pallas_call(
        delta_kernel,
        grid=(1,),
        in_specs=[whole(heads, length, kw), whole(heads, length, kw), whole(heads, length, vw),
                  whole(heads, length, 1), whole(heads, length, 1), whole(heads, n_chunks, CHUNK)],
        out_specs=[whole(heads, length, vw + kw), whole(heads, kw, vw + kw)],
        out_shape=[jax.ShapeDtypeStruct((heads, length, vw + kw), jnp.float32),
                   jax.ShapeDtypeStruct((heads, kw, vw + kw), jnp.float32)],
        name="delta_chunks",
    )(queries, key_rows, values, beta_col, cum_col, cum)


def passed_along(value, axis, steps):
    count = lax.axis_size(axis)
    first, last = (max(0, -steps), min(count, count - steps))
    return lax.ppermute(value, axis, [(source, source + steps) for source in range(first, last)])


def shifted(value, axis, steps):
    count = lax.axis_size(axis)
    return lax.ppermute(value, axis, [(source, source + steps) for source in range(count - steps)])


def batched_mm(a, b):
    return jnp.einsum("hij,hjk->hik", a, b, precision=HI)


def incoming_state(pair, axis):
    count, place = lax.axis_size(axis), lax.axis_index(axis)
    value_width = pair.shape[2] - pair.shape[1]
    offset_lanes = lax.broadcasted_iota(jnp.int32, pair.shape, 2) < value_width
    steps = 1
    while steps < count:
        reached = place >= steps
        transfer = pair[..., value_width:]
        if 2 * steps < count:
            far = shifted(pair, axis, steps)
            joined = batched_mm(transfer, far) + jnp.where(offset_lanes, pair, 0.0)
            pair = jnp.where(reached, joined, pair)
        else:
            far = shifted(pair[..., :value_width], axis, steps)
            offset = pair[..., :value_width]
            offset = jnp.where(reached, offset + batched_mm(transfer, far), offset)
        steps *= 2
    return shifted(offset, axis, 1)


def rms_rows(values, gain):
    values = values.astype(jnp.float32)
    scale = lax.rsqrt(jnp.mean(values * values, axis=-1, keepdims=True) + epsilon)
    return values * scale * gain


def unit_heads(array, heads):
    reshaped_rows = array.reshape(array.shape[0], heads, -1)
    return reshaped_rows * lax.rsqrt(
        jnp.sum(reshaped_rows * reshaped_rows, axis=-1, keepdims=True) + epsilon
    )


def on_device(
    stream,
    moe_gain,
    router,
    expert_ids,
    expert_gate,
    expert_up,
    expert_down,
    mixer_gain,
    query_weight,
    key_weight,
    value_weight,
    output_gate,
    beta_weight,
    decay_weight,
    query_conv,
    key_conv,
    value_conv,
    decay_log,
    decay_bias,
    head_gain,
    out_weight,
):
    ctx_count = lax.axis_size("ctx")
    head_count = lax.axis_size("head")
    sources = ctx_count * head_count
    tok_rows, model_width = stream.shape
    top_count = expert_ids.shape[1]
    local_experts = expert_gate.shape[0]
    experts_all = local_experts * sources
    capacity = (11 * tok_rows * top_count + 10 * experts_all - 1) // (10 * experts_all)
    normed = rms_rows(stream, moe_gain).astype(jnp.bfloat16)
    logits = jnp.dot(normed, router, preferred_element_type=jnp.float32)
    expert_hit = expert_ids[:, :, None] == jnp.arange(experts_all, dtype=jnp.int32)[None, None, :]
    chosen = jnp.sum(jnp.where(expert_hit, logits[:, None, :], 0.0), axis=2)
    raised = jnp.exp(chosen)
    weights = raised / jnp.sum(raised, axis=1, keepdims=True)
    flat_ids = expert_ids.reshape(-1)
    matches = (flat_ids[:, None] == jnp.arange(experts_all, dtype=jnp.int32)[None, :]).astype(
        jnp.int32
    )
    slot_index = jnp.sum((jnp.cumsum(matches, axis=0) - 1) * matches, axis=1)
    places = flat_ids * capacity + slot_index
    slot_count = experts_all * capacity
    place_rows = places.reshape(tok_rows, top_count)
    slot_ids = jnp.arange(slot_count, dtype=jnp.int32)
    take = jnp.sum((place_rows[None, :, :] == slot_ids[:, None, None]).astype(jnp.float32), axis=2)
    take = take.astype(jnp.bfloat16).reshape(sources, local_experts, capacity, tok_rows)
    outgoing = jnp.einsum(
        "nest,td->nesd", take, normed, preferred_element_type=jnp.float32
    ).astype(jnp.bfloat16)
    received = lax.all_to_all(outgoing, ("ctx", "head"), split_axis=0, concat_axis=0, tiled=True)
    gate_part = jnp.einsum(
        "nesd,edh->nesh", received, expert_gate, preferred_element_type=jnp.float32
    )
    up_part = jnp.einsum("nesd,edh->nesh", received, expert_up, preferred_element_type=jnp.float32)
    hidden = (jax.nn.silu(gate_part) * up_part).astype(jnp.bfloat16)
    returned = lax.all_to_all(
        jnp.einsum(
            "nesh,ehd->nesd", hidden, expert_down, preferred_element_type=jnp.float32
        ).astype(jnp.bfloat16),
        ("ctx", "head"),
        split_axis=0,
        concat_axis=0,
        tiled=True,
    )
    mix = jnp.sum(
        jnp.where(place_rows[:, :, None] == slot_ids[None, None, :], weights[:, :, None], 0.0), axis=1
    )
    mix = mix.reshape(tok_rows, sources, local_experts, capacity)
    moe_out = jnp.einsum(
        "tnes,nesd->td", mix, returned.astype(jnp.float32), precision=HI
    ).astype(jnp.bfloat16)
    mixer_in = rms_rows(
        stream.astype(jnp.float32) + moe_out.astype(jnp.float32), mixer_gain
    ).astype(jnp.bfloat16)
    weight_list = (query_weight, key_weight, value_weight, output_gate, beta_weight, decay_weight)
    piece_rows = lax.all_gather(mixer_in, "head", axis=0, tiled=True)
    projected = jnp.concatenate(
        [jnp.dot(piece_rows, matrix, preferred_element_type=jnp.float32) for matrix in weight_list],
        axis=1,
    )
    row_count = projected.shape[0]
    key_cols = query_weight.shape[1]
    value_cols = value_weight.shape[1]
    head_cols = beta_weight.shape[1]
    conv_cols = 2 * key_cols + value_cols
    qkv_raw = projected[:, :conv_cols].astype(jnp.bfloat16)
    gate_raw = projected[:, conv_cols : conv_cols + value_cols].astype(jnp.bfloat16)
    beta_raw = projected[:, conv_cols + value_cols : conv_cols + value_cols + head_cols]
    decay_raw = projected[:, conv_cols + value_cols + head_cols :]
    taps = jnp.concatenate([query_conv, key_conv, value_conv], axis=1)
    rim_len = taps.shape[0] - 1
    rim_cells = passed_along(qkv_raw[row_count - rim_len :], "ctx", 1)
    extended = jnp.concatenate([rim_cells.astype(jnp.float32), qkv_raw.astype(jnp.float32)], axis=0)
    summed = jnp.zeros((row_count, conv_cols), jnp.float32)
    for shift_index in range(rim_len + 1):
        summed = (
            summed + taps[shift_index][None, :] * extended[shift_index : shift_index + row_count]
        )
    convolved = jax.nn.silu(summed)
    key_width = DK
    key_heads = key_cols // key_width
    group_size = head_cols // key_heads
    queries = unit_heads(convolved[:, :key_cols], key_heads) * key_width ** (-0.5)
    key_rows = unit_heads(convolved[:, key_cols : 2 * key_cols], key_heads)
    values = convolved[:, 2 * key_cols :].reshape(row_count, head_cols, -1)
    strength = jax.nn.sigmoid(beta_raw)
    decays = -jnp.exp(decay_log)[None, :] * jax.nn.softplus(decay_raw + decay_bias[None, :])
    query_heads = jnp.repeat(queries, group_size, axis=1).transpose(1, 0, 2)
    key_head_rows = jnp.repeat(key_rows, group_size, axis=1).transpose(1, 0, 2)
    core_parts, carry = local_delta(
        query_heads, key_head_rows, values.transpose(1, 0, 2), strength.T, decays.T
    )
    incoming_rows = incoming_state(carry, "ctx")
    value_width = values.shape[2]
    delta_core_output = core_parts[..., :value_width] + jnp.einsum(
        "wnc,wcg->wng", core_parts[..., value_width:], incoming_rows, precision=HI
    )
    delta_core_output = delta_core_output.transpose(1, 0, 2)
    normal = (
        delta_core_output
        * lax.rsqrt(
            jnp.mean(delta_core_output * delta_core_output, axis=-1, keepdims=True) + epsilon
        )
        * head_gain
    )
    gate_values = gate_raw.astype(jnp.float32).reshape(row_count, head_cols, -1)
    gated_out = (
        (normal * jax.nn.silu(gate_values)).astype(jnp.bfloat16).reshape(row_count, value_cols)
    )
    mixer_out = lax.psum_scatter(
        jnp.dot(gated_out, out_weight, preferred_element_type=jnp.float32).astype(jnp.bfloat16),
        "head",
        scatter_dimension=0,
        tiled=True,
    )
    return (moe_out, mixer_out)


def solution(mesh):
    return jax.shard_map(
        on_device,
        mesh=mesh,
        in_specs=(
            P(("ctx", "head"), None),
            P(),
            P(),
            P(("ctx", "head"), None),
            P(("ctx", "head"), None, None),
            P(("ctx", "head"), None, None),
            P(("ctx", "head"), None, None),
            P(),
            P(None, "head"),
            P(None, "head"),
            P(None, "head"),
            P(None, "head"),
            P(None, "head"),
            P(None, "head"),
            P(None, "head"),
            P(None, "head"),
            P(None, "head"),
            P("head"),
            P("head"),
            P(),
            P("head", None),
        ),
        out_specs=(P(("ctx", "head"), None), P(("ctx", "head"), None)),
        check_vma=False,
    )
```

```python
import math

import jax
import jax.numpy as jnp
from jax import lax
from jax.experimental import pallas as pl
from jax.experimental.pallas import tpu as pltpu
from jax.sharding import PartitionSpec as P

DK = 128
HI = lax.Precision.HIGHEST
KERNEL_PRECISION = lax.Precision.HIGH
CHUNK = 64
GROUP = 256
epsilon = 1e-06


def _mm(a, b):
    return jnp.dot(a, b, precision=KERNEL_PRECISION, preferred_element_type=jnp.float32)


def _mm_nt(a, b):
    return lax.dot_general(a, b, (((1,), (1,)), ((), ())), precision=KERNEL_PRECISION,
                           preferred_element_type=jnp.float32)


def _mm_tn(a, b):
    return lax.dot_general(a, b, (((0,), (0,)), ((), ())), precision=KERNEL_PRECISION,
                           preferred_element_type=jnp.float32)


def delta_kernel(q_ref, k_ref, v_ref, b_ref, cc_ref, cg_ref, last_ref, out_ref, carry_ref,
                 wv_s, wk_s, qd_s, kd_s, mix_s, change_s, starts_s):
    heads, length, kw = q_ref.shape
    vw = v_ref.shape[2]
    n_chunks = length // CHUNK
    n_groups = length // GROUP
    per_group = GROUP // CHUNK
    row = lax.broadcasted_iota(jnp.int32, (GROUP, GROUP), 0)
    col = lax.broadcasted_iota(jnp.int32, (GROUP, GROUP), 1)
    same = (row // CHUNK) == (col // CHUNK)
    strict = (row > col) & same
    inclusive = (row >= col) & same
    eye_g = jnp.where(row == col, 1.0, 0.0).astype(jnp.float32)
    pairs = ((row // 2) == (col // 2)) & (row != col)
    for h in range(heads):
        for g in range(n_groups):
            rows = pl.ds(g * GROUP, GROUP)
            q = q_ref[h, rows, :]
            k = k_ref[h, rows, :]
            v = v_ref[h, rows, :]
            beta = b_ref[h, rows, :]
            cum_c = cc_ref[h, rows, :]
            cum_r = cg_ref[h, pl.ds(g, 1), :]
            spread = cum_c - cum_r
            fall_s = jnp.where(strict, jnp.exp(jnp.where(strict, spread, 0.0)), 0.0)
            fall_i = jnp.where(inclusive, jnp.exp(jnp.where(inclusive, spread, 0.0)), 0.0)
            a = beta * fall_s * _mm_nt(k, k)
            inv = eye_g - jnp.where(pairs, a, 0.0)
            size = 2
            while size < CHUNK:
                band = ((row // (2 * size)) == (col // (2 * size))) & ((row // size) != (col // size))
                inv = inv - _mm(_mm(inv, jnp.where(band, a, 0.0)), inv)
                size *= 2
            ec = jnp.exp(cum_c)
            solved = _mm(inv, jnp.concatenate([beta * v, (beta * ec) * k], axis=1))
            wv_s[h, rows, :] = solved[:, :vw]
            wk_s[h, rows, :] = solved[:, vw:]
            mix_s[h, rows, :] = fall_i * _mm_nt(q, k)
            qd_s[h, rows, :] = ec * q
            kd_s[h, rows, :] = jnp.exp(last_ref[h, rows, :] - cum_c) * k

    lane = lax.broadcasted_iota(jnp.int32, (CHUNK, vw + kw), 1)
    value_lanes = lane < vw
    krow = lax.broadcasted_iota(jnp.int32, (kw, vw + kw), 0)
    kcol = lax.broadcasted_iota(jnp.int32, (kw, vw + kw), 1)
    carry0 = jnp.where(kcol - vw == krow, 1.0, 0.0).astype(jnp.float32)

    def step(c, carries):
        rows = pl.ds(pl.multiple_of(c * CHUNK, CHUNK), CHUNK)
        new = []
        for h in range(heads):
            carry = carries[h]
            starts_s[h, c] = carry
            w_values = jnp.concatenate([wv_s[h, rows, :], jnp.zeros((CHUNK, kw), jnp.float32)], axis=1)
            change = w_values - _mm(wk_s[h, rows, :], carry)
            change_s[h, rows, :] = change
            closing = jnp.exp(last_ref[h, pl.ds(c * CHUNK, 1), :])
            new.append(closing * carry + _mm_tn(kd_s[h, rows, :], change))
        return tuple(new)

    carries = lax.fori_loop(0, n_chunks, step, (carry0,) * heads)
    for h in range(heads):
        carry_ref[h] = carries[h]
        for g in range(n_groups):
            rows = pl.ds(g * GROUP, GROUP)
            mixed = _mm(mix_s[h, rows, :], change_s[h, rows, :])
            for j in range(per_group):
                c = g * per_group + j
                sub = pl.ds(c * CHUNK, CHUNK)
                out_ref[h, sub, :] = mixed[j * CHUNK:(j + 1) * CHUNK] + _mm(qd_s[h, sub, :], starts_s[h, c])


def local_delta(queries, key_rows, values, strength, decays):
    heads, length, kw = queries.shape
    vw = values.shape[2]
    n_chunks = length // CHUNK
    cum = jnp.cumsum(decays.reshape(heads, n_chunks, CHUNK), axis=-1)
    last = jnp.broadcast_to(cum[..., CHUNK - 1:], cum.shape).reshape(heads, length, 1)
    whole = lambda *shape: pl.BlockSpec(shape, lambda i: (0,) * len(shape))
    return pl.pallas_call(
        delta_kernel,
        grid=(1,),
        in_specs=[whole(heads, length, kw), whole(heads, length, kw), whole(heads, length, vw),
                  whole(heads, length, 1), whole(heads, length, 1),
                  whole(heads, length // GROUP, GROUP), whole(heads, length, 1)],
        out_specs=[whole(heads, length, vw + kw), whole(heads, kw, vw + kw)],
        out_shape=[jax.ShapeDtypeStruct((heads, length, vw + kw), jnp.float32),
                   jax.ShapeDtypeStruct((heads, kw, vw + kw), jnp.float32)],
        scratch_shapes=[pltpu.VMEM((heads, length, vw), jnp.float32),
                        pltpu.VMEM((heads, length, kw), jnp.float32),
                        pltpu.VMEM((heads, length, kw), jnp.float32),
                        pltpu.VMEM((heads, length, kw), jnp.float32),
                        pltpu.VMEM((heads, length, GROUP), jnp.float32),
                        pltpu.VMEM((heads, length, vw + kw), jnp.float32),
                        pltpu.VMEM((heads, n_chunks, kw, vw + kw), jnp.float32)],
        name="delta_chunks",
    )(queries, key_rows, values, strength.reshape(heads, length, 1), cum.reshape(heads, length, 1),
      cum.reshape(heads, length // GROUP, GROUP), last)


def passed_along(value, axis, steps):
    count = lax.axis_size(axis)
    first, last = (max(0, -steps), min(count, count - steps))
    return lax.ppermute(value, axis, [(source, source + steps) for source in range(first, last)])


def shifted(value, axis, steps):
    count = lax.axis_size(axis)
    return lax.ppermute(value, axis, [(source, source + steps) for source in range(count - steps)])


def batched_mm(a, b):
    return jnp.einsum("hij,hjk->hik", a, b, precision=HI)


def incoming_state(pair, axis):
    count, place = lax.axis_size(axis), lax.axis_index(axis)
    value_width = pair.shape[2] - pair.shape[1]
    offset_lanes = lax.broadcasted_iota(jnp.int32, pair.shape, 2) < value_width
    steps = 1
    while steps < count:
        reached = place >= steps
        transfer = pair[..., value_width:]
        if 2 * steps < count:
            far = shifted(pair, axis, steps)
            joined = batched_mm(transfer, far) + jnp.where(offset_lanes, pair, 0.0)
            pair = jnp.where(reached, joined, pair)
        else:
            far = shifted(pair[..., :value_width], axis, steps)
            offset = pair[..., :value_width]
            offset = jnp.where(reached, offset + batched_mm(transfer, far), offset)
        steps *= 2
    return shifted(offset, axis, 1)


def rms_rows(values, gain):
    values = values.astype(jnp.float32)
    scale = lax.rsqrt(jnp.mean(values * values, axis=-1, keepdims=True) + epsilon)
    return values * scale * gain


def unit_heads(array, heads):
    reshaped_rows = array.reshape(array.shape[0], heads, -1)
    return reshaped_rows * lax.rsqrt(
        jnp.sum(reshaped_rows * reshaped_rows, axis=-1, keepdims=True) + epsilon
    )


def on_device(
    stream,
    moe_gain,
    router,
    expert_ids,
    expert_gate,
    expert_up,
    expert_down,
    mixer_gain,
    query_weight,
    key_weight,
    value_weight,
    output_gate,
    beta_weight,
    decay_weight,
    query_conv,
    key_conv,
    value_conv,
    decay_log,
    decay_bias,
    head_gain,
    out_weight,
):
    ctx_count = lax.axis_size("ctx")
    head_count = lax.axis_size("head")
    sources = ctx_count * head_count
    tok_rows, model_width = stream.shape
    top_count = expert_ids.shape[1]
    local_experts = expert_gate.shape[0]
    experts_all = local_experts * sources
    capacity = (11 * tok_rows * top_count + 10 * experts_all - 1) // (10 * experts_all)
    normed = rms_rows(stream, moe_gain).astype(jnp.bfloat16)
    logits = jnp.dot(normed, router, preferred_element_type=jnp.float32)
    expert_hit = expert_ids[:, :, None] == jnp.arange(experts_all, dtype=jnp.int32)[None, None, :]
    chosen = jnp.sum(jnp.where(expert_hit, logits[:, None, :], 0.0), axis=2)
    raised = jnp.exp(chosen)
    weights = raised / jnp.sum(raised, axis=1, keepdims=True)
    flat_ids = expert_ids.reshape(-1)
    matches = (flat_ids[:, None] == jnp.arange(experts_all, dtype=jnp.int32)[None, :]).astype(
        jnp.int32
    )
    slot_index = jnp.sum((jnp.cumsum(matches, axis=0) - 1) * matches, axis=1)
    places = flat_ids * capacity + slot_index
    slot_count = experts_all * capacity
    place_rows = places.reshape(tok_rows, top_count)
    slot_ids = jnp.arange(slot_count, dtype=jnp.int32)
    take = jnp.sum((place_rows[None, :, :] == slot_ids[:, None, None]).astype(jnp.float32), axis=2)
    take = take.astype(jnp.bfloat16).reshape(sources, local_experts, capacity, tok_rows)
    outgoing = jnp.einsum(
        "nest,td->nesd", take, normed, preferred_element_type=jnp.float32
    ).astype(jnp.bfloat16)
    received = lax.all_to_all(outgoing, ("ctx", "head"), split_axis=0, concat_axis=0, tiled=True)
    gate_part = jnp.einsum(
        "nesd,edh->nesh", received, expert_gate, preferred_element_type=jnp.float32
    )
    up_part = jnp.einsum("nesd,edh->nesh", received, expert_up, preferred_element_type=jnp.float32)
    hidden = (jax.nn.silu(gate_part) * up_part).astype(jnp.bfloat16)
    returned = lax.all_to_all(
        jnp.einsum(
            "nesh,ehd->nesd", hidden, expert_down, preferred_element_type=jnp.float32
        ).astype(jnp.bfloat16),
        ("ctx", "head"),
        split_axis=0,
        concat_axis=0,
        tiled=True,
    )
    mix = jnp.sum(
        jnp.where(place_rows[:, :, None] == slot_ids[None, None, :], weights[:, :, None], 0.0), axis=1
    )
    mix = mix.reshape(tok_rows, sources, local_experts, capacity)
    moe_out = jnp.einsum(
        "tnes,nesd->td", mix, returned.astype(jnp.float32), precision=HI
    ).astype(jnp.bfloat16)
    mixer_in = rms_rows(
        stream.astype(jnp.float32) + moe_out.astype(jnp.float32), mixer_gain
    ).astype(jnp.bfloat16)
    weight_list = (query_weight, key_weight, value_weight, output_gate, beta_weight, decay_weight)
    piece_rows = lax.all_gather(mixer_in, "head", axis=0, tiled=True)
    projected = jnp.concatenate(
        [jnp.dot(piece_rows, matrix, preferred_element_type=jnp.float32) for matrix in weight_list],
        axis=1,
    )
    row_count = projected.shape[0]
    key_cols = query_weight.shape[1]
    value_cols = value_weight.shape[1]
    head_cols = beta_weight.shape[1]
    conv_cols = 2 * key_cols + value_cols
    qkv_raw = projected[:, :conv_cols].astype(jnp.bfloat16)
    gate_raw = projected[:, conv_cols : conv_cols + value_cols].astype(jnp.bfloat16)
    beta_raw = projected[:, conv_cols + value_cols : conv_cols + value_cols + head_cols]
    decay_raw = projected[:, conv_cols + value_cols + head_cols :]
    taps = jnp.concatenate([query_conv, key_conv, value_conv], axis=1)
    rim_len = taps.shape[0] - 1
    rim_cells = passed_along(qkv_raw[row_count - rim_len :], "ctx", 1)
    extended = jnp.concatenate([rim_cells.astype(jnp.float32), qkv_raw.astype(jnp.float32)], axis=0)
    summed = jnp.zeros((row_count, conv_cols), jnp.float32)
    for shift_index in range(rim_len + 1):
        summed = (
            summed + taps[shift_index][None, :] * extended[shift_index : shift_index + row_count]
        )
    convolved = jax.nn.silu(summed)
    key_width = DK
    key_heads = key_cols // key_width
    group_size = head_cols // key_heads
    queries = unit_heads(convolved[:, :key_cols], key_heads) * key_width ** (-0.5)
    key_rows = unit_heads(convolved[:, key_cols : 2 * key_cols], key_heads)
    values = convolved[:, 2 * key_cols :].reshape(row_count, head_cols, -1)
    strength = jax.nn.sigmoid(beta_raw)
    decays = -jnp.exp(decay_log)[None, :] * jax.nn.softplus(decay_raw + decay_bias[None, :])
    query_heads = jnp.repeat(queries, group_size, axis=1).transpose(1, 0, 2)
    key_head_rows = jnp.repeat(key_rows, group_size, axis=1).transpose(1, 0, 2)
    core_parts, carry = local_delta(
        query_heads, key_head_rows, values.transpose(1, 0, 2), strength.T, decays.T
    )
    incoming_rows = incoming_state(carry, "ctx")
    value_width = values.shape[2]
    delta_core_output = core_parts[..., :value_width] + jnp.einsum(
        "wnc,wcg->wng", core_parts[..., value_width:], incoming_rows, precision=HI
    )
    delta_core_output = delta_core_output.transpose(1, 0, 2)
    normal = (
        delta_core_output
        * lax.rsqrt(
            jnp.mean(delta_core_output * delta_core_output, axis=-1, keepdims=True) + epsilon
        )
        * head_gain
    )
    gate_values = gate_raw.astype(jnp.float32).reshape(row_count, head_cols, -1)
    gated_out = (
        (normal * jax.nn.silu(gate_values)).astype(jnp.bfloat16).reshape(row_count, value_cols)
    )
    mixer_out = lax.psum_scatter(
        jnp.dot(gated_out, out_weight, preferred_element_type=jnp.float32).astype(jnp.bfloat16),
        "head",
        scatter_dimension=0,
        tiled=True,
    )
    return (moe_out, mixer_out)


def solution(mesh):
    return jax.shard_map(
        on_device,
        mesh=mesh,
        in_specs=(
            P(("ctx", "head"), None),
            P(),
            P(),
            P(("ctx", "head"), None),
            P(("ctx", "head"), None, None),
            P(("ctx", "head"), None, None),
            P(("ctx", "head"), None, None),
            P(),
            P(None, "head"),
            P(None, "head"),
            P(None, "head"),
            P(None, "head"),
            P(None, "head"),
            P(None, "head"),
            P(None, "head"),
            P(None, "head"),
            P(None, "head"),
            P("head"),
            P("head"),
            P(),
            P("head", None),
        ),
        out_specs=(P(("ctx", "head"), None), P(("ctx", "head"), None)),
        check_vma=False,
    )
```

```python
import math

import jax
import jax.numpy as jnp
from jax import lax
from jax.experimental import pallas as pl
from jax.experimental.pallas import tpu as pltpu
from jax.sharding import PartitionSpec as P

DK = 128
HI = lax.Precision.HIGHEST
KERNEL_PRECISION = lax.Precision.HIGH
CHUNK = 64
GROUP = 256
epsilon = 1e-06


def _mm(a, b):
    return jnp.dot(a, b, precision=KERNEL_PRECISION, preferred_element_type=jnp.float32)


def _mm_nt(a, b):
    return lax.dot_general(a, b, (((1,), (1,)), ((), ())), precision=KERNEL_PRECISION,
                           preferred_element_type=jnp.float32)


def _mm_tn(a, b):
    return lax.dot_general(a, b, (((0,), (0,)), ((), ())), precision=KERNEL_PRECISION,
                           preferred_element_type=jnp.float32)


def delta_kernel(q_ref, k_ref, v_ref, b_ref, cc_ref, cg_ref, last_ref, out_ref, carry_ref,
                 wv_s, wk_s, qd_s, kd_s, mix_s, change_s, starts_s):
    heads, length, kw = q_ref.shape
    vw = v_ref.shape[2]
    n_chunks = length // CHUNK
    n_groups = length // GROUP
    per_group = GROUP // CHUNK
    row = lax.broadcasted_iota(jnp.int32, (GROUP, GROUP), 0)
    col = lax.broadcasted_iota(jnp.int32, (GROUP, GROUP), 1)
    same = (row // CHUNK) == (col // CHUNK)
    strict = (row > col) & same
    inclusive = (row >= col) & same
    eye_g = jnp.where(row == col, 1.0, 0.0).astype(jnp.float32)
    pairs = ((row // 2) == (col // 2)) & (row != col)
    for h in range(heads):
        for g in range(n_groups):
            rows = pl.ds(g * GROUP, GROUP)
            q = q_ref[h, rows, :]
            k = k_ref[h, rows, :]
            v = v_ref[h, rows, :]
            beta = b_ref[h, rows, :]
            cum_c = cc_ref[h, rows, :]
            cum_r = cg_ref[h, pl.ds(g, 1), :]
            spread = cum_c - cum_r
            fall_s = jnp.where(strict, jnp.exp(jnp.where(strict, spread, 0.0)), 0.0)
            fall_i = jnp.where(inclusive, jnp.exp(jnp.where(inclusive, spread, 0.0)), 0.0)
            a = beta * fall_s * _mm_nt(k, k)
            inv = eye_g - jnp.where(pairs, a, 0.0)
            size = 2
            while size < CHUNK:
                band = ((row // (2 * size)) == (col // (2 * size))) & ((row // size) != (col // size))
                inv = inv - _mm(_mm(inv, jnp.where(band, a, 0.0)), inv)
                size *= 2
            ec = jnp.exp(cum_c)
            solved = _mm(inv, jnp.concatenate([beta * v, (beta * ec) * k], axis=1))
            wv_s[h, rows, :] = solved[:, :vw]
            wk_s[h, rows, :] = solved[:, vw:]
            mix_s[h, rows, :] = fall_i * _mm_nt(q, k)
            qd_s[h, rows, :] = ec * q
            kd_s[h, rows, :] = jnp.exp(last_ref[h, rows, :] - cum_c) * k

    lane = lax.broadcasted_iota(jnp.int32, (CHUNK, vw + kw), 1)
    value_lanes = lane < vw
    krow = lax.broadcasted_iota(jnp.int32, (kw, vw + kw), 0)
    kcol = lax.broadcasted_iota(jnp.int32, (kw, vw + kw), 1)
    carry0 = jnp.where(kcol - vw == krow, 1.0, 0.0).astype(jnp.float32)

    def step(c, carries):
        rows = pl.ds(pl.multiple_of(c * CHUNK, CHUNK), CHUNK)
        new = []
        for h in range(heads):
            carry = carries[h]
            starts_s[h, c] = carry
            w_values = jnp.concatenate([wv_s[h, rows, :], jnp.zeros((CHUNK, kw), jnp.float32)], axis=1)
            change = w_values - _mm(wk_s[h, rows, :], carry)
            change_s[h, rows, :] = change
            closing = jnp.exp(last_ref[h, pl.ds(c * CHUNK, 1), :])
            new.append(closing * carry + _mm_tn(kd_s[h, rows, :], change))
        return tuple(new)

    carries = lax.fori_loop(0, n_chunks, step, (carry0,) * heads)
    for h in range(heads):
        carry_ref[h] = carries[h]
        for g in range(n_groups):
            rows = pl.ds(g * GROUP, GROUP)
            mixed = _mm(mix_s[h, rows, :], change_s[h, rows, :])
            for j in range(per_group):
                c = g * per_group + j
                sub = pl.ds(c * CHUNK, CHUNK)
                out_ref[h, sub, :] = mixed[j * CHUNK:(j + 1) * CHUNK] + _mm(qd_s[h, sub, :], starts_s[h, c])


def local_delta(queries, key_rows, values, strength, decays):
    heads, length, kw = queries.shape
    vw = values.shape[2]
    n_chunks = length // CHUNK
    cum = jnp.cumsum(decays.reshape(heads, n_chunks, CHUNK), axis=-1)
    last = jnp.broadcast_to(cum[..., CHUNK - 1:], cum.shape).reshape(heads, length, 1)
    whole = lambda *shape: pl.BlockSpec(shape, lambda i: (0,) * len(shape))
    return pl.pallas_call(
        delta_kernel,
        grid=(1,),
        in_specs=[whole(heads, length, kw), whole(heads, length, kw), whole(heads, length, vw),
                  whole(heads, length, 1), whole(heads, length, 1),
                  whole(heads, length // GROUP, GROUP), whole(heads, length, 1)],
        out_specs=[whole(heads, length, vw + kw), whole(heads, kw, vw + kw)],
        out_shape=[jax.ShapeDtypeStruct((heads, length, vw + kw), jnp.float32),
                   jax.ShapeDtypeStruct((heads, kw, vw + kw), jnp.float32)],
        scratch_shapes=[pltpu.VMEM((heads, length, vw), jnp.float32),
                        pltpu.VMEM((heads, length, kw), jnp.float32),
                        pltpu.VMEM((heads, length, kw), jnp.float32),
                        pltpu.VMEM((heads, length, kw), jnp.float32),
                        pltpu.VMEM((heads, length, GROUP), jnp.float32),
                        pltpu.VMEM((heads, length, vw + kw), jnp.float32),
                        pltpu.VMEM((heads, n_chunks, kw, vw + kw), jnp.float32)],
        name="delta_chunks",
    )(queries, key_rows, values, strength.reshape(heads, length, 1), cum.reshape(heads, length, 1),
      cum.reshape(heads, length // GROUP, GROUP), last)


def passed_along(value, axis, steps):
    count = lax.axis_size(axis)
    first, last = (max(0, -steps), min(count, count - steps))
    return lax.ppermute(value, axis, [(source, source + steps) for source in range(first, last)])


def shifted(value, axis, steps):
    count = lax.axis_size(axis)
    return lax.ppermute(value, axis, [(source, source + steps) for source in range(count - steps)])


def batched_mm(a, b):
    return jnp.einsum("hij,hjk->hik", a, b, precision=HI)


def incoming_state(pair, axis):
    count, place = lax.axis_size(axis), lax.axis_index(axis)
    value_width = pair.shape[2] - pair.shape[1]
    offset_lanes = lax.broadcasted_iota(jnp.int32, pair.shape, 2) < value_width
    steps = 1
    while steps < count:
        reached = place >= steps
        transfer = pair[..., value_width:]
        if 2 * steps < count:
            far = shifted(pair, axis, steps)
            joined = batched_mm(transfer, far) + jnp.where(offset_lanes, pair, 0.0)
            pair = jnp.where(reached, joined, pair)
        else:
            far = shifted(pair[..., :value_width], axis, steps)
            offset = pair[..., :value_width]
            offset = jnp.where(reached, offset + batched_mm(transfer, far), offset)
        steps *= 2
    return shifted(offset, axis, 1)


def rms_rows(values, gain):
    values = values.astype(jnp.float32)
    scale = lax.rsqrt(jnp.mean(values * values, axis=-1, keepdims=True) + epsilon)
    return values * scale * gain


def unit_heads(array, heads):
    reshaped_rows = array.reshape(array.shape[0], heads, -1)
    return reshaped_rows * lax.rsqrt(
        jnp.sum(reshaped_rows * reshaped_rows, axis=-1, keepdims=True) + epsilon
    )


def on_device(
    stream,
    moe_gain,
    router,
    expert_ids,
    expert_gate,
    expert_up,
    expert_down,
    mixer_gain,
    query_weight,
    key_weight,
    value_weight,
    output_gate,
    beta_weight,
    decay_weight,
    query_conv,
    key_conv,
    value_conv,
    decay_log,
    decay_bias,
    head_gain,
    out_weight,
):
    ctx_count = lax.axis_size("ctx")
    head_count = lax.axis_size("head")
    sources = ctx_count * head_count
    tok_rows, model_width = stream.shape
    top_count = expert_ids.shape[1]
    local_experts = expert_gate.shape[0]
    experts_all = local_experts * sources
    capacity = (11 * tok_rows * top_count + 10 * experts_all - 1) // (10 * experts_all)
    normed = rms_rows(stream, moe_gain).astype(jnp.bfloat16)
    logits = jnp.dot(normed, router, preferred_element_type=jnp.float32)
    expert_hit = expert_ids[:, :, None] == jnp.arange(experts_all, dtype=jnp.int32)[None, None, :]
    chosen = jnp.sum(jnp.where(expert_hit, logits[:, None, :], 0.0), axis=2)
    raised = jnp.exp(chosen)
    weights = raised / jnp.sum(raised, axis=1, keepdims=True)
    flat_ids = expert_ids.reshape(-1)
    matches = (flat_ids[:, None] == jnp.arange(experts_all, dtype=jnp.int32)[None, :]).astype(
        jnp.int32
    )
    slot_index = jnp.sum((jnp.cumsum(matches, axis=0) - 1) * matches, axis=1)
    places = flat_ids * capacity + slot_index
    slot_count = experts_all * capacity
    place_rows = places.reshape(tok_rows, top_count)
    slot_ids = jnp.arange(slot_count, dtype=jnp.int32)
    take = jnp.sum((place_rows[None, :, :] == slot_ids[:, None, None]).astype(jnp.float32), axis=2)
    take = take.astype(jnp.bfloat16).reshape(sources, local_experts, capacity, tok_rows)
    outgoing = jnp.einsum(
        "nest,td->nesd", take, normed, preferred_element_type=jnp.float32
    ).astype(jnp.bfloat16)
    received = lax.all_to_all(outgoing, ("ctx", "head"), split_axis=0, concat_axis=0, tiled=True)
    gate_part = jnp.einsum(
        "nesd,edh->nesh", received, expert_gate, preferred_element_type=jnp.float32
    )
    up_part = jnp.einsum("nesd,edh->nesh", received, expert_up, preferred_element_type=jnp.float32)
    hidden = (jax.nn.silu(gate_part) * up_part).astype(jnp.bfloat16)
    returned = lax.all_to_all(
        jnp.einsum(
            "nesh,ehd->nesd", hidden, expert_down, preferred_element_type=jnp.float32
        ).astype(jnp.bfloat16),
        ("ctx", "head"),
        split_axis=0,
        concat_axis=0,
        tiled=True,
    )
    mix = jnp.sum(
        jnp.where(place_rows[:, :, None] == slot_ids[None, None, :], weights[:, :, None], 0.0), axis=1
    )
    mix = mix.reshape(tok_rows, sources, local_experts, capacity)
    mix_high = mix.astype(jnp.bfloat16)
    mix_low = (mix - mix_high.astype(jnp.float32)).astype(jnp.bfloat16)
    both = jnp.einsum(
        "tnes,nesd->td",
        jnp.concatenate([mix_high, mix_low], axis=0),
        returned,
        preferred_element_type=jnp.float32,
    )
    moe_out = (both[:tok_rows] + both[tok_rows:]).astype(jnp.bfloat16)
    mixer_in = rms_rows(
        stream.astype(jnp.float32) + moe_out.astype(jnp.float32), mixer_gain
    ).astype(jnp.bfloat16)
    weight_list = (query_weight, key_weight, value_weight, output_gate, beta_weight, decay_weight)
    piece_rows = lax.all_gather(mixer_in, "head", axis=0, tiled=True)
    projected = jnp.concatenate(
        [jnp.dot(piece_rows, matrix, preferred_element_type=jnp.float32) for matrix in weight_list],
        axis=1,
    )
    row_count = projected.shape[0]
    key_cols = query_weight.shape[1]
    value_cols = value_weight.shape[1]
    head_cols = beta_weight.shape[1]
    conv_cols = 2 * key_cols + value_cols
    qkv_raw = projected[:, :conv_cols].astype(jnp.bfloat16)
    gate_raw = projected[:, conv_cols : conv_cols + value_cols].astype(jnp.bfloat16)
    beta_raw = projected[:, conv_cols + value_cols : conv_cols + value_cols + head_cols]
    decay_raw = projected[:, conv_cols + value_cols + head_cols :]
    taps = jnp.concatenate([query_conv, key_conv, value_conv], axis=1)
    rim_len = taps.shape[0] - 1
    rim_cells = passed_along(qkv_raw[row_count - rim_len :], "ctx", 1)
    extended = jnp.concatenate([rim_cells.astype(jnp.float32), qkv_raw.astype(jnp.float32)], axis=0)
    summed = jnp.zeros((row_count, conv_cols), jnp.float32)
    for shift_index in range(rim_len + 1):
        summed = (
            summed + taps[shift_index][None, :] * extended[shift_index : shift_index + row_count]
        )
    convolved = jax.nn.silu(summed)
    key_width = DK
    key_heads = key_cols // key_width
    group_size = head_cols // key_heads
    queries = unit_heads(convolved[:, :key_cols], key_heads) * key_width ** (-0.5)
    key_rows = unit_heads(convolved[:, key_cols : 2 * key_cols], key_heads)
    values = convolved[:, 2 * key_cols :].reshape(row_count, head_cols, -1)
    strength = jax.nn.sigmoid(beta_raw)
    decays = -jnp.exp(decay_log)[None, :] * jax.nn.softplus(decay_raw + decay_bias[None, :])
    query_heads = jnp.repeat(queries, group_size, axis=1).transpose(1, 0, 2)
    key_head_rows = jnp.repeat(key_rows, group_size, axis=1).transpose(1, 0, 2)
    core_parts, carry = local_delta(
        query_heads, key_head_rows, values.transpose(1, 0, 2), strength.T, decays.T
    )
    incoming_rows = incoming_state(carry, "ctx")
    value_width = values.shape[2]
    delta_core_output = core_parts[..., :value_width] + jnp.einsum(
        "wnc,wcg->wng", core_parts[..., value_width:], incoming_rows, precision=HI
    )
    delta_core_output = delta_core_output.transpose(1, 0, 2)
    normal = (
        delta_core_output
        * lax.rsqrt(
            jnp.mean(delta_core_output * delta_core_output, axis=-1, keepdims=True) + epsilon
        )
        * head_gain
    )
    gate_values = gate_raw.astype(jnp.float32).reshape(row_count, head_cols, -1)
    gated_out = (
        (normal * jax.nn.silu(gate_values)).astype(jnp.bfloat16).reshape(row_count, value_cols)
    )
    mixer_out = lax.psum_scatter(
        jnp.dot(gated_out, out_weight, preferred_element_type=jnp.float32).astype(jnp.bfloat16),
        "head",
        scatter_dimension=0,
        tiled=True,
    )
    return (moe_out, mixer_out)


def solution(mesh):
    return jax.shard_map(
        on_device,
        mesh=mesh,
        in_specs=(
            P(("ctx", "head"), None),
            P(),
            P(),
            P(("ctx", "head"), None),
            P(("ctx", "head"), None, None),
            P(("ctx", "head"), None, None),
            P(("ctx", "head"), None, None),
            P(),
            P(None, "head"),
            P(None, "head"),
            P(None, "head"),
            P(None, "head"),
            P(None, "head"),
            P(None, "head"),
            P(None, "head"),
            P(None, "head"),
            P(None, "head"),
            P("head"),
            P("head"),
            P(),
            P("head", None),
        ),
        out_specs=(P(("ctx", "head"), None), P(("ctx", "head"), None)),
        check_vma=False,
    )
```

```python
import math

import jax
import jax.numpy as jnp
from jax import lax
from jax.experimental import pallas as pl
from jax.experimental.pallas import tpu as pltpu
from jax.sharding import PartitionSpec as P

DK = 128
HI = lax.Precision.HIGHEST
KERNEL_PRECISION = lax.Precision.HIGH
CHUNK = 64
GROUP = 256
epsilon = 1e-06


def _mm(a, b):
    return jnp.dot(a, b, precision=KERNEL_PRECISION, preferred_element_type=jnp.float32)


def _mm_nt(a, b):
    return lax.dot_general(a, b, (((1,), (1,)), ((), ())), precision=KERNEL_PRECISION,
                           preferred_element_type=jnp.float32)


def _mm_tn(a, b):
    return lax.dot_general(a, b, (((0,), (0,)), ((), ())), precision=KERNEL_PRECISION,
                           preferred_element_type=jnp.float32)


def delta_kernel(q_ref, k_ref, v_ref, b_ref, cc_ref, cg_ref, last_ref, out_ref, carry_ref,
                 wv_s, wk_s, qd_s, kd_s, mix_s, change_s, starts_s):
    heads, length, kw = q_ref.shape
    vw = v_ref.shape[2]
    n_chunks = length // CHUNK
    n_groups = length // GROUP
    per_group = GROUP // CHUNK
    row = lax.broadcasted_iota(jnp.int32, (GROUP, GROUP), 0)
    col = lax.broadcasted_iota(jnp.int32, (GROUP, GROUP), 1)
    same = (row // CHUNK) == (col // CHUNK)
    strict = (row > col) & same
    inclusive = (row >= col) & same
    eye_g = jnp.where(row == col, 1.0, 0.0).astype(jnp.float32)
    pairs = ((row // 2) == (col // 2)) & (row != col)
    for h in range(heads):
        for g in range(n_groups):
            rows = pl.ds(g * GROUP, GROUP)
            q = q_ref[h, rows, :]
            k = k_ref[h, rows, :]
            v = v_ref[h, rows, :]
            beta = b_ref[h, rows, :]
            cum_c = cc_ref[h, rows, :]
            cum_r = cg_ref[h, pl.ds(g, 1), :]
            spread = cum_c - cum_r
            fall_s = jnp.where(strict, jnp.exp(jnp.where(strict, spread, 0.0)), 0.0)
            fall_i = jnp.where(inclusive, jnp.exp(jnp.where(inclusive, spread, 0.0)), 0.0)
            a = beta * fall_s * _mm_nt(k, k)
            inv = eye_g - jnp.where(pairs, a, 0.0)
            size = 2
            while size < CHUNK:
                band = ((row // (2 * size)) == (col // (2 * size))) & ((row // size) != (col // size))
                inv = inv - _mm(_mm(inv, jnp.where(band, a, 0.0)), inv)
                size *= 2
            ec = jnp.exp(cum_c)
            solved = _mm(inv, jnp.concatenate([beta * v, (beta * ec) * k], axis=1))
            wv_s[h, rows, :] = solved[:, :vw]
            wk_s[h, rows, :] = solved[:, vw:]
            mix_s[h, rows, :] = fall_i * _mm_nt(q, k)
            qd_s[h, rows, :] = ec * q
            kd_s[h, rows, :] = jnp.exp(last_ref[h, rows, :] - cum_c) * k

    lane = lax.broadcasted_iota(jnp.int32, (CHUNK, vw + kw), 1)
    value_lanes = lane < vw
    krow = lax.broadcasted_iota(jnp.int32, (kw, vw + kw), 0)
    kcol = lax.broadcasted_iota(jnp.int32, (kw, vw + kw), 1)
    carry0 = jnp.where(kcol - vw == krow, 1.0, 0.0).astype(jnp.float32)

    def step(c, carries):
        rows = pl.ds(pl.multiple_of(c * CHUNK, CHUNK), CHUNK)
        new = []
        for h in range(heads):
            carry = carries[h]
            starts_s[h, c] = carry
            w_values = jnp.concatenate([wv_s[h, rows, :], jnp.zeros((CHUNK, kw), jnp.float32)], axis=1)
            change = w_values - _mm(wk_s[h, rows, :], carry)
            change_s[h, rows, :] = change
            closing = jnp.exp(last_ref[h, pl.ds(c * CHUNK, 1), :])
            new.append(closing * carry + _mm_tn(kd_s[h, rows, :], change))
        return tuple(new)

    carries = lax.fori_loop(0, n_chunks, step, (carry0,) * heads)
    for h in range(heads):
        carry_ref[h] = carries[h]
        for g in range(n_groups):
            rows = pl.ds(g * GROUP, GROUP)
            mixed = _mm(mix_s[h, rows, :], change_s[h, rows, :])
            for j in range(per_group):
                c = g * per_group + j
                sub = pl.ds(c * CHUNK, CHUNK)
                out_ref[h, sub, :] = mixed[j * CHUNK:(j + 1) * CHUNK] + _mm(qd_s[h, sub, :], starts_s[h, c])


def local_delta(queries, key_rows, values, strength, decays):
    heads, length, kw = queries.shape
    vw = values.shape[2]
    n_chunks = length // CHUNK
    cum = jnp.cumsum(decays.reshape(heads, n_chunks, CHUNK), axis=-1)
    last = jnp.broadcast_to(cum[..., CHUNK - 1:], cum.shape).reshape(heads, length, 1)
    whole = lambda *shape: pl.BlockSpec(shape, lambda i: (0,) * len(shape))
    return pl.pallas_call(
        delta_kernel,
        grid=(1,),
        in_specs=[whole(heads, length, kw), whole(heads, length, kw), whole(heads, length, vw),
                  whole(heads, length, 1), whole(heads, length, 1),
                  whole(heads, length // GROUP, GROUP), whole(heads, length, 1)],
        out_specs=[whole(heads, length, vw + kw), whole(heads, kw, vw + kw)],
        out_shape=[jax.ShapeDtypeStruct((heads, length, vw + kw), jnp.float32),
                   jax.ShapeDtypeStruct((heads, kw, vw + kw), jnp.float32)],
        scratch_shapes=[pltpu.VMEM((heads, length, vw), jnp.float32),
                        pltpu.VMEM((heads, length, kw), jnp.float32),
                        pltpu.VMEM((heads, length, kw), jnp.float32),
                        pltpu.VMEM((heads, length, kw), jnp.float32),
                        pltpu.VMEM((heads, length, GROUP), jnp.float32),
                        pltpu.VMEM((heads, length, vw + kw), jnp.float32),
                        pltpu.VMEM((heads, n_chunks, kw, vw + kw), jnp.float32)],
        name="delta_chunks",
    )(queries, key_rows, values, strength.reshape(heads, length, 1), cum.reshape(heads, length, 1),
      cum.reshape(heads, length // GROUP, GROUP), last)


def passed_along(value, axis, steps):
    count = lax.axis_size(axis)
    first, last = (max(0, -steps), min(count, count - steps))
    return lax.ppermute(value, axis, [(source, source + steps) for source in range(first, last)])


def shifted(value, axis, steps):
    count = lax.axis_size(axis)
    return lax.ppermute(value, axis, [(source, source + steps) for source in range(count - steps)])


def batched_mm(a, b):
    return jnp.einsum("hij,hjk->hik", a, b, precision=HI)


def incoming_state(pair, axis):
    count, place = lax.axis_size(axis), lax.axis_index(axis)
    value_width = pair.shape[2] - pair.shape[1]
    offset_lanes = lax.broadcasted_iota(jnp.int32, pair.shape, 2) < value_width
    steps = 1
    while steps < count:
        reached = place >= steps
        transfer = pair[..., value_width:]
        if 2 * steps < count:
            far = shifted(pair, axis, steps)
            joined = batched_mm(transfer, far) + jnp.where(offset_lanes, pair, 0.0)
            pair = jnp.where(reached, joined, pair)
        else:
            far = shifted(pair[..., :value_width], axis, steps)
            offset = pair[..., :value_width]
            offset = jnp.where(reached, offset + batched_mm(transfer, far), offset)
        steps *= 2
    return shifted(offset, axis, 1)


def rms_rows(values, gain):
    values = values.astype(jnp.float32)
    scale = lax.rsqrt(jnp.mean(values * values, axis=-1, keepdims=True) + epsilon)
    return values * scale * gain


def unit_heads(array, heads):
    reshaped_rows = array.reshape(array.shape[0], heads, -1)
    return reshaped_rows * lax.rsqrt(
        jnp.sum(reshaped_rows * reshaped_rows, axis=-1, keepdims=True) + epsilon
    )


def on_device(
    stream,
    moe_gain,
    router,
    expert_ids,
    expert_gate,
    expert_up,
    expert_down,
    mixer_gain,
    query_weight,
    key_weight,
    value_weight,
    output_gate,
    beta_weight,
    decay_weight,
    query_conv,
    key_conv,
    value_conv,
    decay_log,
    decay_bias,
    head_gain,
    out_weight,
):
    ctx_count = lax.axis_size("ctx")
    head_count = lax.axis_size("head")
    sources = ctx_count * head_count
    tok_rows, model_width = stream.shape
    top_count = expert_ids.shape[1]
    local_experts = expert_gate.shape[0]
    experts_all = local_experts * sources
    capacity = (11 * tok_rows * top_count + 10 * experts_all - 1) // (10 * experts_all)
    normed = rms_rows(stream, moe_gain).astype(jnp.bfloat16)
    logits = jnp.dot(normed, router, preferred_element_type=jnp.float32)
    expert_hit = expert_ids[:, :, None] == jnp.arange(experts_all, dtype=jnp.int32)[None, None, :]
    chosen = jnp.sum(jnp.where(expert_hit, logits[:, None, :], 0.0), axis=2)
    raised = jnp.exp(chosen)
    weights = raised / jnp.sum(raised, axis=1, keepdims=True)
    flat_ids = expert_ids.reshape(-1)
    matches = (flat_ids[:, None] == jnp.arange(experts_all, dtype=jnp.int32)[None, :]).astype(
        jnp.int32
    )
    slot_index = jnp.sum((jnp.cumsum(matches, axis=0) - 1) * matches, axis=1)
    places = flat_ids * capacity + slot_index
    slot_count = experts_all * capacity
    place_rows = places.reshape(tok_rows, top_count)
    slot_ids = jnp.arange(slot_count, dtype=jnp.int32)
    take = jnp.sum((place_rows[None, :, :] == slot_ids[:, None, None]).astype(jnp.float32), axis=2)
    take = take.astype(jnp.bfloat16).reshape(sources, local_experts, capacity, tok_rows)
    outgoing = jnp.einsum(
        "nest,td->nesd", take, normed, preferred_element_type=jnp.float32
    ).astype(jnp.bfloat16)
    received = lax.all_to_all(outgoing, ("ctx", "head"), split_axis=0, concat_axis=0, tiled=True)
    gate_part = jnp.einsum(
        "nesd,edh->nesh", received, expert_gate, preferred_element_type=jnp.float32
    )
    up_part = jnp.einsum("nesd,edh->nesh", received, expert_up, preferred_element_type=jnp.float32)
    hidden = (jax.nn.silu(gate_part) * up_part).astype(jnp.bfloat16)
    returned = lax.all_to_all(
        jnp.einsum(
            "nesh,ehd->nesd", hidden, expert_down, preferred_element_type=jnp.float32
        ).astype(jnp.bfloat16),
        ("ctx", "head"),
        split_axis=0,
        concat_axis=0,
        tiled=True,
    )
    mix = jnp.sum(
        jnp.where(place_rows[:, :, None] == slot_ids[None, None, :], weights[:, :, None], 0.0), axis=1
    )
    mix = mix.reshape(tok_rows, sources, local_experts, capacity)
    mix_rounded = lax.reduce_precision(mix, exponent_bits=8, mantissa_bits=7)
    mix_high = mix_rounded.astype(jnp.bfloat16)
    mix_low = (mix - mix_rounded).astype(jnp.bfloat16)
    both = jnp.einsum(
        "tnes,nesd->td",
        jnp.concatenate([mix_high, mix_low], axis=0),
        returned,
        preferred_element_type=jnp.float32,
    )
    moe_out = (both[:tok_rows] + both[tok_rows:]).astype(jnp.bfloat16)
    mixer_in = rms_rows(
        stream.astype(jnp.float32) + moe_out.astype(jnp.float32), mixer_gain
    ).astype(jnp.bfloat16)
    weight_list = (query_weight, key_weight, value_weight, output_gate, beta_weight, decay_weight)
    piece_rows = lax.all_gather(mixer_in, "head", axis=0, tiled=True)
    projected = jnp.concatenate(
        [jnp.dot(piece_rows, matrix, preferred_element_type=jnp.float32) for matrix in weight_list],
        axis=1,
    )
    row_count = projected.shape[0]
    key_cols = query_weight.shape[1]
    value_cols = value_weight.shape[1]
    head_cols = beta_weight.shape[1]
    conv_cols = 2 * key_cols + value_cols
    qkv_raw = projected[:, :conv_cols].astype(jnp.bfloat16)
    gate_raw = projected[:, conv_cols : conv_cols + value_cols].astype(jnp.bfloat16)
    beta_raw = projected[:, conv_cols + value_cols : conv_cols + value_cols + head_cols]
    decay_raw = projected[:, conv_cols + value_cols + head_cols :]
    taps = jnp.concatenate([query_conv, key_conv, value_conv], axis=1)
    rim_len = taps.shape[0] - 1
    rim_cells = passed_along(qkv_raw[row_count - rim_len :], "ctx", 1)
    extended = jnp.concatenate([rim_cells.astype(jnp.float32), qkv_raw.astype(jnp.float32)], axis=0)
    summed = jnp.zeros((row_count, conv_cols), jnp.float32)
    for shift_index in range(rim_len + 1):
        summed = (
            summed + taps[shift_index][None, :] * extended[shift_index : shift_index + row_count]
        )
    convolved = jax.nn.silu(summed)
    key_width = DK
    key_heads = key_cols // key_width
    group_size = head_cols // key_heads
    queries = unit_heads(convolved[:, :key_cols], key_heads) * key_width ** (-0.5)
    key_rows = unit_heads(convolved[:, key_cols : 2 * key_cols], key_heads)
    values = convolved[:, 2 * key_cols :].reshape(row_count, head_cols, -1)
    strength = jax.nn.sigmoid(beta_raw)
    decays = -jnp.exp(decay_log)[None, :] * jax.nn.softplus(decay_raw + decay_bias[None, :])
    query_heads = jnp.repeat(queries, group_size, axis=1).transpose(1, 0, 2)
    key_head_rows = jnp.repeat(key_rows, group_size, axis=1).transpose(1, 0, 2)
    core_parts, carry = local_delta(
        query_heads, key_head_rows, values.transpose(1, 0, 2), strength.T, decays.T
    )
    incoming_rows = incoming_state(carry, "ctx")
    value_width = values.shape[2]
    delta_core_output = core_parts[..., :value_width] + jnp.einsum(
        "wnc,wcg->wng", core_parts[..., value_width:], incoming_rows, precision=HI
    )
    delta_core_output = delta_core_output.transpose(1, 0, 2)
    normal = (
        delta_core_output
        * lax.rsqrt(
            jnp.mean(delta_core_output * delta_core_output, axis=-1, keepdims=True) + epsilon
        )
        * head_gain
    )
    gate_values = gate_raw.astype(jnp.float32).reshape(row_count, head_cols, -1)
    gated_out = (
        (normal * jax.nn.silu(gate_values)).astype(jnp.bfloat16).reshape(row_count, value_cols)
    )
    mixer_out = lax.psum_scatter(
        jnp.dot(gated_out, out_weight, preferred_element_type=jnp.float32).astype(jnp.bfloat16),
        "head",
        scatter_dimension=0,
        tiled=True,
    )
    return (moe_out, mixer_out)


def solution(mesh):
    return jax.shard_map(
        on_device,
        mesh=mesh,
        in_specs=(
            P(("ctx", "head"), None),
            P(),
            P(),
            P(("ctx", "head"), None),
            P(("ctx", "head"), None, None),
            P(("ctx", "head"), None, None),
            P(("ctx", "head"), None, None),
            P(),
            P(None, "head"),
            P(None, "head"),
            P(None, "head"),
            P(None, "head"),
            P(None, "head"),
            P(None, "head"),
            P(None, "head"),
            P(None, "head"),
            P(None, "head"),
            P("head"),
            P("head"),
            P(),
            P("head", None),
        ),
        out_specs=(P(("ctx", "head"), None), P(("ctx", "head"), None)),
        check_vma=False,
    )
```

```python
import math

import jax
import jax.numpy as jnp
from jax import lax
from jax.experimental import pallas as pl
from jax.experimental.pallas import tpu as pltpu
from jax.sharding import PartitionSpec as P

DK = 128
HI = lax.Precision.HIGHEST
KERNEL_PRECISION = lax.Precision.HIGH
CHUNK = 64
GROUP = 256
epsilon = 1e-06


def _mm(a, b):
    return jnp.dot(a, b, precision=KERNEL_PRECISION, preferred_element_type=jnp.float32)


def _mm_nt(a, b):
    return lax.dot_general(a, b, (((1,), (1,)), ((), ())), precision=KERNEL_PRECISION,
                           preferred_element_type=jnp.float32)


def _mm_tn(a, b):
    return lax.dot_general(a, b, (((0,), (0,)), ((), ())), precision=KERNEL_PRECISION,
                           preferred_element_type=jnp.float32)


def delta_kernel(q_ref, k_ref, v_ref, b_ref, cc_ref, cg_ref, last_ref, out_ref, carry_ref,
                 wv_s, wk_s, qd_s, kd_s, mix_s, change_s, starts_s):
    heads, length, kw = q_ref.shape
    vw = v_ref.shape[2]
    n_chunks = length // CHUNK
    n_groups = length // GROUP
    per_group = GROUP // CHUNK
    row = lax.broadcasted_iota(jnp.int32, (GROUP, GROUP), 0)
    col = lax.broadcasted_iota(jnp.int32, (GROUP, GROUP), 1)
    same = (row // CHUNK) == (col // CHUNK)
    strict = (row > col) & same
    inclusive = (row >= col) & same
    eye_g = jnp.where(row == col, 1.0, 0.0).astype(jnp.float32)
    pairs = ((row // 2) == (col // 2)) & (row != col)
    for h in range(heads):
        for g in range(n_groups):
            rows = pl.ds(g * GROUP, GROUP)
            q = q_ref[h, rows, :]
            k = k_ref[h, rows, :]
            v = v_ref[h, rows, :]
            beta = b_ref[h, rows, :]
            cum_c = cc_ref[h, rows, :]
            cum_r = cg_ref[h, pl.ds(g, 1), :]
            spread = cum_c - cum_r
            fall_s = jnp.where(strict, jnp.exp(jnp.where(strict, spread, 0.0)), 0.0)
            fall_i = jnp.where(inclusive, jnp.exp(jnp.where(inclusive, spread, 0.0)), 0.0)
            a = beta * fall_s * _mm_nt(k, k)
            inv = eye_g - jnp.where(pairs, a, 0.0)
            size = 2
            while size < CHUNK:
                band = ((row // (2 * size)) == (col // (2 * size))) & ((row // size) != (col // size))
                inv = inv - _mm(_mm(inv, jnp.where(band, a, 0.0)), inv)
                size *= 2
            ec = jnp.exp(cum_c)
            solved = _mm(inv, jnp.concatenate([beta * v, (beta * ec) * k], axis=1))
            wv_s[h, rows, :] = solved[:, :vw]
            wk_s[h, rows, :] = solved[:, vw:]
            mix_s[h, rows, :] = fall_i * _mm_nt(q, k)
            qd_s[h, rows, :] = ec * q
            kd_s[h, rows, :] = jnp.exp(last_ref[h, rows, :] - cum_c) * k

    lane = lax.broadcasted_iota(jnp.int32, (CHUNK, vw + kw), 1)
    value_lanes = lane < vw
    krow = lax.broadcasted_iota(jnp.int32, (kw, vw + kw), 0)
    kcol = lax.broadcasted_iota(jnp.int32, (kw, vw + kw), 1)
    carry0 = jnp.where(kcol - vw == krow, 1.0, 0.0).astype(jnp.float32)

    def step(c, carries):
        rows = pl.ds(pl.multiple_of(c * CHUNK, CHUNK), CHUNK)
        new = []
        for h in range(heads):
            carry = carries[h]
            starts_s[h, c] = carry
            w_values = jnp.concatenate([wv_s[h, rows, :], jnp.zeros((CHUNK, kw), jnp.float32)], axis=1)
            change = w_values - _mm(wk_s[h, rows, :], carry)
            change_s[h, rows, :] = change
            closing = jnp.exp(last_ref[h, pl.ds(c * CHUNK, 1), :])
            new.append(closing * carry + _mm_tn(kd_s[h, rows, :], change))
        return tuple(new)

    carries = lax.fori_loop(0, n_chunks, step, (carry0,) * heads)
    for h in range(heads):
        carry_ref[h] = carries[h]
        for g in range(n_groups):
            rows = pl.ds(g * GROUP, GROUP)
            mixed = _mm(mix_s[h, rows, :], change_s[h, rows, :])
            for j in range(per_group):
                c = g * per_group + j
                sub = pl.ds(c * CHUNK, CHUNK)
                out_ref[h, sub, :] = mixed[j * CHUNK:(j + 1) * CHUNK] + _mm(qd_s[h, sub, :], starts_s[h, c])


def local_delta(queries, key_rows, values, strength, decays):
    heads, length, kw = queries.shape
    vw = values.shape[2]
    n_chunks = length // CHUNK
    cum = jnp.cumsum(decays.reshape(heads, n_chunks, CHUNK), axis=-1)
    last = jnp.broadcast_to(cum[..., CHUNK - 1:], cum.shape).reshape(heads, length, 1)
    whole = lambda *shape: pl.BlockSpec(shape, lambda i: (0,) * len(shape))
    return pl.pallas_call(
        delta_kernel,
        grid=(1,),
        in_specs=[whole(heads, length, kw), whole(heads, length, kw), whole(heads, length, vw),
                  whole(heads, length, 1), whole(heads, length, 1),
                  whole(heads, length // GROUP, GROUP), whole(heads, length, 1)],
        out_specs=[whole(heads, length, vw + kw), whole(heads, kw, vw + kw)],
        out_shape=[jax.ShapeDtypeStruct((heads, length, vw + kw), jnp.float32),
                   jax.ShapeDtypeStruct((heads, kw, vw + kw), jnp.float32)],
        scratch_shapes=[pltpu.VMEM((heads, length, vw), jnp.float32),
                        pltpu.VMEM((heads, length, kw), jnp.float32),
                        pltpu.VMEM((heads, length, kw), jnp.float32),
                        pltpu.VMEM((heads, length, kw), jnp.float32),
                        pltpu.VMEM((heads, length, GROUP), jnp.float32),
                        pltpu.VMEM((heads, length, vw + kw), jnp.float32),
                        pltpu.VMEM((heads, n_chunks, kw, vw + kw), jnp.float32)],
        name="delta_chunks",
    )(queries, key_rows, values, strength.reshape(heads, length, 1), cum.reshape(heads, length, 1),
      cum.reshape(heads, length // GROUP, GROUP), last)


def passed_along(value, axis, steps):
    count = lax.axis_size(axis)
    first, last = (max(0, -steps), min(count, count - steps))
    return lax.ppermute(value, axis, [(source, source + steps) for source in range(first, last)])


def shifted(value, axis, steps):
    count = lax.axis_size(axis)
    return lax.ppermute(value, axis, [(source, source + steps) for source in range(count - steps)])


def batched_mm(a, b):
    return jnp.einsum("hij,hjk->hik", a, b, precision=HI)


def incoming_state(pair, axis):
    count, place = lax.axis_size(axis), lax.axis_index(axis)
    value_width = pair.shape[2] - pair.shape[1]
    offset_lanes = lax.broadcasted_iota(jnp.int32, pair.shape, 2) < value_width
    steps = 1
    while steps < count:
        reached = place >= steps
        transfer = pair[..., value_width:]
        if 2 * steps < count:
            far = shifted(pair.astype(jnp.bfloat16), axis, steps).astype(jnp.float32)
            joined = batched_mm(transfer, far) + jnp.where(offset_lanes, pair, 0.0)
            pair = jnp.where(reached, joined, pair)
        else:
            far = shifted(pair[..., :value_width].astype(jnp.bfloat16), axis, steps).astype(jnp.float32)
            offset = pair[..., :value_width]
            offset = jnp.where(reached, offset + batched_mm(transfer, far), offset)
        steps *= 2
    return shifted(offset.astype(jnp.bfloat16), axis, 1).astype(jnp.float32)


def rms_rows(values, gain):
    values = values.astype(jnp.float32)
    scale = lax.rsqrt(jnp.mean(values * values, axis=-1, keepdims=True) + epsilon)
    return values * scale * gain


def unit_heads(array, heads):
    reshaped_rows = array.reshape(array.shape[0], heads, -1)
    return reshaped_rows * lax.rsqrt(
        jnp.sum(reshaped_rows * reshaped_rows, axis=-1, keepdims=True) + epsilon
    )


def on_device(
    stream,
    moe_gain,
    router,
    expert_ids,
    expert_gate,
    expert_up,
    expert_down,
    mixer_gain,
    query_weight,
    key_weight,
    value_weight,
    output_gate,
    beta_weight,
    decay_weight,
    query_conv,
    key_conv,
    value_conv,
    decay_log,
    decay_bias,
    head_gain,
    out_weight,
):
    ctx_count = lax.axis_size("ctx")
    head_count = lax.axis_size("head")
    sources = ctx_count * head_count
    tok_rows, model_width = stream.shape
    top_count = expert_ids.shape[1]
    local_experts = expert_gate.shape[0]
    experts_all = local_experts * sources
    capacity = (11 * tok_rows * top_count + 10 * experts_all - 1) // (10 * experts_all)
    normed = rms_rows(stream, moe_gain).astype(jnp.bfloat16)
    logits = jnp.dot(normed, router, preferred_element_type=jnp.float32)
    expert_hit = expert_ids[:, :, None] == jnp.arange(experts_all, dtype=jnp.int32)[None, None, :]
    chosen = jnp.sum(jnp.where(expert_hit, logits[:, None, :], 0.0), axis=2)
    raised = jnp.exp(chosen)
    weights = raised / jnp.sum(raised, axis=1, keepdims=True)
    flat_ids = expert_ids.reshape(-1)
    matches = (flat_ids[:, None] == jnp.arange(experts_all, dtype=jnp.int32)[None, :]).astype(
        jnp.int32
    )
    slot_index = jnp.sum((jnp.cumsum(matches, axis=0) - 1) * matches, axis=1)
    places = flat_ids * capacity + slot_index
    slot_count = experts_all * capacity
    place_rows = places.reshape(tok_rows, top_count)
    slot_ids = jnp.arange(slot_count, dtype=jnp.int32)
    take = jnp.sum((place_rows[None, :, :] == slot_ids[:, None, None]).astype(jnp.float32), axis=2)
    take = take.astype(jnp.bfloat16).reshape(sources, local_experts, capacity, tok_rows)
    outgoing = jnp.einsum(
        "nest,td->nesd", take, normed, preferred_element_type=jnp.float32
    ).astype(jnp.bfloat16)
    received = lax.all_to_all(outgoing, ("ctx", "head"), split_axis=0, concat_axis=0, tiled=True)
    gate_part = jnp.einsum(
        "nesd,edh->nesh", received, expert_gate, preferred_element_type=jnp.float32
    )
    up_part = jnp.einsum("nesd,edh->nesh", received, expert_up, preferred_element_type=jnp.float32)
    hidden = (jax.nn.silu(gate_part) * up_part).astype(jnp.bfloat16)
    returned = lax.all_to_all(
        jnp.einsum(
            "nesh,ehd->nesd", hidden, expert_down, preferred_element_type=jnp.float32
        ).astype(jnp.bfloat16),
        ("ctx", "head"),
        split_axis=0,
        concat_axis=0,
        tiled=True,
    )
    mix = jnp.sum(
        jnp.where(place_rows[:, :, None] == slot_ids[None, None, :], weights[:, :, None], 0.0), axis=1
    )
    mix = mix.reshape(tok_rows, sources, local_experts, capacity)
    mix_rounded = lax.reduce_precision(mix, exponent_bits=8, mantissa_bits=7)
    mix_high = mix_rounded.astype(jnp.bfloat16)
    mix_low = (mix - mix_rounded).astype(jnp.bfloat16)
    both = jnp.einsum(
        "tnes,nesd->td",
        jnp.concatenate([mix_high, mix_low], axis=0),
        returned,
        preferred_element_type=jnp.float32,
    )
    moe_out = (both[:tok_rows] + both[tok_rows:]).astype(jnp.bfloat16)
    mixer_in = rms_rows(
        stream.astype(jnp.float32) + moe_out.astype(jnp.float32), mixer_gain
    ).astype(jnp.bfloat16)
    weight_list = (query_weight, key_weight, value_weight, output_gate, beta_weight, decay_weight)
    piece_rows = lax.all_gather(mixer_in, "head", axis=0, tiled=True)
    projected = jnp.concatenate(
        [jnp.dot(piece_rows, matrix, preferred_element_type=jnp.float32) for matrix in weight_list],
        axis=1,
    )
    row_count = projected.shape[0]
    key_cols = query_weight.shape[1]
    value_cols = value_weight.shape[1]
    head_cols = beta_weight.shape[1]
    conv_cols = 2 * key_cols + value_cols
    qkv_raw = projected[:, :conv_cols].astype(jnp.bfloat16)
    gate_raw = projected[:, conv_cols : conv_cols + value_cols].astype(jnp.bfloat16)
    beta_raw = projected[:, conv_cols + value_cols : conv_cols + value_cols + head_cols]
    decay_raw = projected[:, conv_cols + value_cols + head_cols :]
    taps = jnp.concatenate([query_conv, key_conv, value_conv], axis=1)
    rim_len = taps.shape[0] - 1
    rim_cells = passed_along(qkv_raw[row_count - rim_len :], "ctx", 1)
    extended = jnp.concatenate([rim_cells.astype(jnp.float32), qkv_raw.astype(jnp.float32)], axis=0)
    summed = jnp.zeros((row_count, conv_cols), jnp.float32)
    for shift_index in range(rim_len + 1):
        summed = (
            summed + taps[shift_index][None, :] * extended[shift_index : shift_index + row_count]
        )
    convolved = jax.nn.silu(summed)
    key_width = DK
    key_heads = key_cols // key_width
    group_size = head_cols // key_heads
    queries = unit_heads(convolved[:, :key_cols], key_heads) * key_width ** (-0.5)
    key_rows = unit_heads(convolved[:, key_cols : 2 * key_cols], key_heads)
    values = convolved[:, 2 * key_cols :].reshape(row_count, head_cols, -1)
    strength = jax.nn.sigmoid(beta_raw)
    decays = -jnp.exp(decay_log)[None, :] * jax.nn.softplus(decay_raw + decay_bias[None, :])
    query_heads = jnp.repeat(queries, group_size, axis=1).transpose(1, 0, 2)
    key_head_rows = jnp.repeat(key_rows, group_size, axis=1).transpose(1, 0, 2)
    core_parts, carry = local_delta(
        query_heads, key_head_rows, values.transpose(1, 0, 2), strength.T, decays.T
    )
    incoming_rows = incoming_state(carry, "ctx")
    value_width = values.shape[2]
    delta_core_output = core_parts[..., :value_width] + jnp.einsum(
        "wnc,wcg->wng", core_parts[..., value_width:], incoming_rows, precision=HI
    )
    delta_core_output = delta_core_output.transpose(1, 0, 2)
    normal = (
        delta_core_output
        * lax.rsqrt(
            jnp.mean(delta_core_output * delta_core_output, axis=-1, keepdims=True) + epsilon
        )
        * head_gain
    )
    gate_values = gate_raw.astype(jnp.float32).reshape(row_count, head_cols, -1)
    gated_out = (
        (normal * jax.nn.silu(gate_values)).astype(jnp.bfloat16).reshape(row_count, value_cols)
    )
    mixer_out = lax.psum_scatter(
        jnp.dot(gated_out, out_weight, preferred_element_type=jnp.float32).astype(jnp.bfloat16),
        "head",
        scatter_dimension=0,
        tiled=True,
    )
    return (moe_out, mixer_out)


def solution(mesh):
    return jax.shard_map(
        on_device,
        mesh=mesh,
        in_specs=(
            P(("ctx", "head"), None),
            P(),
            P(),
            P(("ctx", "head"), None),
            P(("ctx", "head"), None, None),
            P(("ctx", "head"), None, None),
            P(("ctx", "head"), None, None),
            P(),
            P(None, "head"),
            P(None, "head"),
            P(None, "head"),
            P(None, "head"),
            P(None, "head"),
            P(None, "head"),
            P(None, "head"),
            P(None, "head"),
            P(None, "head"),
            P("head"),
            P("head"),
            P(),
            P("head", None),
        ),
        out_specs=(P(("ctx", "head"), None), P(("ctx", "head"), None)),
        check_vma=False,
    )
```
